256 devices in a mesh: row: 32 (over z, x), col: 8 (over y, core).
Axes of the slice: x: 4, y: 4, z: 8, core: 2. Of those that a mesh axis runs over, the one named last changes fastest.
Arguments:
- trail_grad: bfloat16 [16384, 16384], P('row', 'col'), may hold values from -6 to 6
- panel_factor: bfloat16 [16384, 1024], P('col'), may hold values from -0.046875 to 0.046875
- cross_factor: bfloat16 [512, 512], replicated, may hold values from -0.25 to 0.25
- diag_factor: bfloat16 [2, 512, 512], replicated, may hold values from -1 to 3, as said below
- diag_inverse: float32 [2, 512, 512], replicated, may hold values from -2 to 2, as said below
- panel_grad: bfloat16 [16384, 1024], P('row'), may hold values from -6 to 6
- cross_grad: bfloat16 [512, 512], replicated, may hold values from -6 to 6
- diag_grad: bfloat16 [2, 512, 512], replicated, may hold values from -6 to 6
Outputs:
- panel_adj: float32 [16384, 1024], P('row', 'col')
- cross_adj: float32 [512, 512], P('col')
- diag_adj: float32 [2, 512, 512], P(None, 'col')
The draws below stay inside these ranges and needn't reach their ends.
Inputs may be any that keep to these rules, and one draw needn't show every extreme that they name: Each diag_factor[p] is lower triangular with a positive diagonal. diag_inverse[p] is the float32 inverse of diag_factor[p], lower triangular.
All inputs are finite; a program needn't handle non-finite values.
Results may differ from the reference program's by a relative error of at most 0.0003.
Values may be sent and summed in bfloat16 or wider, within the bound.
A program may use at most 128 MiB of HBM per device.

```python
import math
import jax
import jax.numpy as jnp
from jax import lax

NT = 16384
B = 512


def diag_pair(key):
    folded = jax.random.fold_in(key, 7)
    key_scale, key_strict = jax.random.split(folded)
    scales = jax.random.uniform(key_scale, (2, B), minval=1.0, maxval=2.0)
    strict = jax.random.normal(key_strict, (2, B, B)) * (0.5 / math.sqrt(B))
    strict = jnp.clip(strict, -0.9, 0.9)
    lower = jnp.tril(strict, -1) + scales[:, :, None] * jnp.eye(B, dtype=jnp.float32)[None, :, :]
    factor_block = lower.astype(jnp.bfloat16)
    inverse_block = jnp.tril(jnp.linalg.inv(factor_block.astype(jnp.float32)))
    return (factor_block, inverse_block)


def draw_diag_factor(key, part):
    return diag_pair(key)[0]


def draw_diag_inverse(key, part):
    return diag_pair(key)[1]


def levels(stream_key, extent, cuts, least, high):
    loudness, own = 1.0, jax.random.fold_in(stream_key, 6)
    for dim, blocks in cuts:
        steps = jnp.exp(jax.random.uniform(jax.random.fold_in(own, dim), (blocks,), jnp.float32, least / len(cuts), high / len(cuts)))
        loudness = loudness * jnp.repeat(steps, extent[dim] // blocks).reshape([-1 if axis == dim else 1 for axis in range(len(extent))])
    return loudness


def normal_values(own_key, shape, spread, reach, shards=(), held_as=jnp.bfloat16):
    values = spread * jax.random.normal(own_key, shape, jnp.float32)
    if shards:
        values = values * levels(own_key, shape, shards, -0.22, 0.18)
    return jnp.clip(values, -reach, reach).astype(held_as)


def setup_inputs(seed: int = 0) -> dict:
    seeds = jax.random.split(jax.random.key(seed), 9)
    trail_grad = normal_values(seeds[0], (NT, NT), 1.0, 6.0, ((0, 32), (1, 8)))
    panel_factor = normal_values(seeds[1], (NT, 2 * B), NT ** -0.5, 0.046875, ((0, 8),))
    cross_factor = normal_values(seeds[2], (B, B), B ** -0.5, 0.25)
    diag_factor = draw_diag_factor(jax.random.fold_in(seeds[8], 71), 0)
    diag_inverse = draw_diag_inverse(jax.random.fold_in(seeds[8], 71), 0)
    panel_grad = normal_values(seeds[5], (NT, 2 * B), 1.0, 6.0, ((0, 32),))
    cross_grad = normal_values(seeds[6], (B, B), 1.0, 6.0)
    diag_grad = normal_values(seeds[7], (2, B, B), 1.0, 6.0)
    return {"trail_grad": trail_grad, "panel_factor": panel_factor, "cross_factor": cross_factor, "diag_factor": diag_factor, "diag_inverse": diag_inverse, "panel_grad": panel_grad, "cross_grad": cross_grad, "diag_grad": diag_grad}


def halve_lower(matrix):
    size = matrix.shape[0]
    row_ids = jnp.arange(size, dtype=jnp.int32)[:, None]
    col_ids = jnp.arange(size, dtype=jnp.int32)[None, :]
    return jnp.where(col_ids < row_ids, matrix, jnp.where(col_ids == row_ids, matrix * 0.5, jnp.zeros_like(matrix)))

def inner_rows(left_mat, right_mat):
    return lax.dot_general(left_mat, right_mat, (((0,), (0,)), ((), ())), precision=lax.Precision.HIGHEST)

def block_adjoint(factor_block, inverse_block, gradient):
    highest = lax.Precision.HIGHEST
    product = inner_rows(factor_block.astype(jnp.float32), gradient)
    halved = halve_lower(product)
    symmetric = halved + halved.T
    inner = inner_rows(inverse_block, symmetric)
    return jnp.dot(inner, inverse_block, precision=highest)

def reference(trail_grad, panel_factor, cross_factor, diag_factor, diag_inverse, panel_grad, cross_grad, diag_grad):
    highest = lax.Precision.HIGHEST
    panel_width = cross_factor.shape[0]
    lower_half = halve_lower(trail_grad.astype(jnp.float32))
    factor_all = panel_factor.astype(jnp.float32)
    trail_term = jnp.dot(lower_half, factor_all, precision=highest) + inner_rows(lower_half, factor_all)
    grads = panel_grad.astype(jnp.float32)
    adj_one = jnp.dot(grads[:, panel_width:] - trail_term[:, panel_width:], diag_inverse[1], precision=highest)
    grad_one = diag_grad[1].astype(jnp.float32) - inner_rows(adj_one, factor_all[:, panel_width:])
    coupled = inner_rows(adj_one, factor_all[:, :panel_width])
    block_one = block_adjoint(diag_factor[1], diag_inverse[1], grad_one)
    cross_f = cross_factor.astype(jnp.float32)
    rest = grads[:, :panel_width] - trail_term[:, :panel_width] - jnp.dot(adj_one, cross_f, precision=highest)
    cross_rest = cross_grad.astype(jnp.float32) - coupled - jnp.dot(block_one, cross_f, precision=highest)
    adj_zero = jnp.dot(rest, diag_inverse[0], precision=highest)
    cross_adj = jnp.dot(cross_rest, diag_inverse[0], precision=highest)
    grad_zero = diag_grad[0].astype(jnp.float32) - inner_rows(adj_zero, factor_all[:, :panel_width]) - inner_rows(cross_adj, cross_f)
    block_zero = block_adjoint(diag_factor[0], diag_inverse[0], grad_zero)
    return (jnp.concatenate([adj_zero, adj_one], axis=1), cross_adj, jnp.stack([block_zero, block_one]))
```

```python
import functools

import jax
import jax.numpy as jnp
from jax import lax
from jax.experimental import pallas as pl
from jax.experimental.pallas import tpu as pltpu
from jax.sharding import Mesh
from jax.sharding import PartitionSpec as P

MESH = pl.DeviceIdType.MESH
F32, BF16 = jnp.float32, jnp.bfloat16
BLOCK = 512
VMEM_BYTES = 56 * 1024 * 1024


def place():
    return tuple(lax.axis_index(a) for a in ("z", "x", "y", "k"))


def meet(peers):
    barrier = pltpu.get_barrier_semaphore()
    for peer in peers:
        pl.semaphore_signal(barrier, inc=1, device_id=peer, device_id_type=MESH)
    pl.semaphore_wait(barrier, len(peers))


def push(src, dst, send, recv, peer):
    return pltpu.make_async_remote_copy(
        src_ref=src, dst_ref=dst, send_sem=send, recv_sem=recv, device_id=peer, device_id_type=MESH
    )


def dot(a, b, ca=1, cb=0):
    return lax.dot_general(a, b, (((ca,), (cb,)), ((), ())), preferred_element_type=F32)


def split(a):
    high = a.astype(BF16)
    return high, (a - high.astype(F32)).astype(BF16)


def dot3(a, b, ca=1, cb=0):
    ah, al = a if isinstance(a, tuple) else split(a)
    bh, bl = b if isinstance(b, tuple) else split(b)
    return dot(ah, bh, ca, cb) + (dot(al, bh, ca, cb) + dot(ah, bl, ca, cb))


def dot2(a, b, ca=1, cb=0):
    if isinstance(a, tuple):
        return dot(a[0], b, ca, cb) + dot(a[1], b, ca, cb)
    return dot(a, b[0], ca, cb) + dot(a, b[1], ca, cb)


def symmetric(f):
    size = f.shape[0]
    rows = lax.broadcasted_iota(jnp.int32, (size, size), 0)
    cols = lax.broadcasted_iota(jnp.int32, (size, size), 1)
    halved = jnp.where(cols < rows, f, jnp.where(cols == rows, f * 0.5, 0.0))
    return halved + halved.T


def exchange_kernel(trail, fac, mx, fz, xs, xr, fs, fr, hs, hr, own_sem):
    z, x, y, k = place()
    c = 2 * y + k
    ys, ks = z >> 1, z & 1
    yn = (lax.rem(y + 3, 4), lax.rem(y + 1, 4))
    xp = [lax.rem(x + d, 4) for d in (1, 2, 3)]
    sibling = (z, x, y, 1 - k)
    meet(
        [(z, p, y, k) for p in xp]
        + [(z, x, yn[s], j) for s in (0, 1) for j in (0, 1)]
        + [sibling]
    )
    lower = c <= z

    def rows(s, i):
        block = lax.rem(x + i // 2, 4)
        return pl.ds(pl.multiple_of(block * BLOCK + s * 256 + (i % 2) * 128, 128), 128)

    def across(d):
        return push(
            trail.at[:, pl.ds(pl.multiple_of(xp[d] * BLOCK, 128), BLOCK)],
            mx.at[pl.ds(pl.multiple_of(x * BLOCK, BLOCK), BLOCK), :],
            xs.at[d],
            xr.at[d],
            (z, xp[d], y, k),
        )

    own_block = pltpu.make_async_copy(
        trail.at[:, pl.ds(pl.multiple_of(x * BLOCK, 128), BLOCK)],
        mx.at[pl.ds(pl.multiple_of(x * BLOCK, BLOCK), BLOCK), :],
        own_sem,
    )
    source_chip = y == ys
    source = source_chip & (k == ks)

    def first_hop(s, i):
        return push(
            fac.at[rows(s, i), :], fz.at[rows(s, i), :], fs.at[s, i], fr.at[i], (z, x, yn[s], s)
        )

    def beside_own(i):
        return push(fac.at[rows(1 - k, i), :], fz.at[rows(1 - k, i), :], hs.at[0, i], fr.at[i], sibling)

    def beside_other(i):
        return push(fac.at[rows(k, i), :], fz.at[rows(k, i), :], hs.at[1, i], hr.at[i], sibling)

    @pl.when(source)
    def _():
        for i in range(8):
            first_hop(0, i).start()
            first_hop(1, i).start()
            beside_own(i).start()
            beside_other(i).start()

    @pl.when(lower)
    def _():
        for d in range(3):
            across(d).start()
        own_block.start()

    onward = jnp.where(k == 0, yn[0], yn[1])
    hops = jnp.where(k == 0, (ys - y + 4) & 3, (y - ys + 4) & 3)

    def forward(i):
        return push(
            fz.at[rows(k, i), :], fz.at[rows(k, i), :], fs.at[0, i], fr.at[i], (z, x, onward, k)
        )

    def share(i):
        return push(fz.at[rows(k, i), :], fz.at[rows(k, i), :], hs.at[0, i], hr.at[i], sibling)

    def other(i):
        return push(fz.at[rows(1 - k, i), :], fz.at[rows(1 - k, i), :], hs.at[0, i], hr.at[i], sibling)

    @pl.when(jnp.logical_not(source_chip))
    def _():
        for i in range(8):
            forward(i).wait_recv()

            @pl.when(hops < 3)
            def _():
                forward(i).start()

            share(i).start()
        for i in range(8):
            other(i).wait_recv()
            share(i).wait_send()

        @pl.when(hops < 3)
        def _():
            for i in range(8):
                forward(i).wait_send()

    @pl.when(source_chip & (k != ks))
    def _():
        for i in range(8):
            forward(i).wait_recv()
            other(i).wait_recv()

    @pl.when(source)
    def _():
        for i in range(8):
            first_hop(0, i).wait_send()
            first_hop(1, i).wait_send()
            beside_own(i).wait_send()
            beside_other(i).wait_send()

    @pl.when(lower)
    def _():
        for d in range(3):
            across(d).wait()
        own_block.wait()


def masked(m, row0, col0):
    rows = row0 + lax.broadcasted_iota(jnp.int32, m.shape, 0)
    cols = col0 + lax.broadcasted_iota(jnp.int32, m.shape, 1)
    scale = jnp.where(cols < rows, 1.0, jnp.where(cols == rows, 0.5, 0.0))
    return (m.astype(F32) * scale).astype(BF16)


def sums_kernel(
    trail, fac, fz, grad, xf, lf, li, cg, dg,
    cross_out, diag_out, mf_out, ph_out, pl_out,
    m, w, full, r0, r1, r2, r3, lit,
    s0, v0, s1, v1, s2, v2, s3, v3, g3, u3, g2, u2, g1, u1, g0, u0,
):
    z, x, y, k = place()
    c = 2 * y + k
    sibling = (z, x, y, 1 - k)
    first = jnp.where(k == 0, y, x)
    second = jnp.where(k == 0, x, y)

    def along_first(p):
        return (z, jnp.where(k == 0, x, p), jnp.where(k == 0, p, y), k)

    def along_second(p):
        return (z, jnp.where(k == 0, p, x), jnp.where(k == 0, y, p), k)

    p1 = [lax.rem(first + d, 4) for d in (1, 2, 3)]
    p2 = [lax.rem(second + d, 4) for d in (1, 2, 3)]
    pz = [lax.rem(z + d, 8) for d in range(1, 8)]
    meet(
        [sibling]
        + [along_first(p) for p in p1]
        + [along_second(p) for p in p2]
        + [(p, x, y, k) for p in pz]
    )

    @pl.when(c <= z)
    def _():
        @pl.loop(0, 4)
        def _(i):
            here = pl.ds(pl.multiple_of(i * 128, 128), 128)
            m[here, :] = trail[here, :]

            @pl.when(c == z)
            def _():
                m[here, :] = masked(trail[here, :], x * BLOCK + i * 128, 0)

            mf_out[here, :] = dot(m[here, :], fac[...])

        mine = pl.ds(pl.multiple_of(x * BLOCK, BLOCK), BLOCK)
        f = jnp.where(c == z, fac[mine, :].astype(F32), fz[mine, :].astype(F32)).astype(BF16)
        own = jnp.where(c == z, 1.0, 0.0)

        def store(block, value):
            for j in range(4):
                w[pl.ds(j * 1536 + block * BLOCK, BLOCK), :] = value[:, j * 128 : (j + 1) * 128]

        for block, (a, b) in enumerate(((1, 1), (1, 0), (0, 0))):
            mfa = mf_out[:, a * BLOCK : (a + 1) * BLOCK]
            mfb = mf_out[:, b * BLOCK : (b + 1) * BLOCK]
            ga = grad[:, a * BLOCK : (a + 1) * BLOCK].astype(F32) * own
            fa = f[:, a * BLOCK : (a + 1) * BLOCK]
            fb = f[:, b * BLOCK : (b + 1) * BLOCK]
            store(block, dot2(split(ga - mfa), fb, 0, 0) - dot2(fa, split(mfb), 0, 0))

    @pl.when(c > z)
    def _():
        mf_out[...] = jnp.zeros_like(mf_out)
        w[...] = jnp.zeros_like(w)

    half = k * 3072

    def part(at, n):
        return pl.ds(pl.multiple_of(at, 8), n)

    c0 = push(w.at[part(3072 - half, 3072), :], r0, s0, v0, sibling)
    c0.start()
    li0, li1 = split(li[0]), split(li[1])
    lf0, lf1, xb = lf[0], lf[1], xf[...]
    j1 = split(dot2(li1, lf1))
    j0 = split(dot2(li0, lf0))
    e1 = dot(lf1, dg[1], 0, 0)
    e0 = dot(lf0, dg[0], 0, 0)
    b1f = dot3(split(dot2(li1, xb)), li0)
    b1 = split(b1f)
    b2 = split(dot2(b1, lf0))
    cj = dot2(cg[...], j0)
    lit[0] = li[0].T
    lit[1] = li[1].T
    ph_out[0:BLOCK, 0:BLOCK], pl_out[0:BLOCK, 0:BLOCK] = li0
    ph_out[BLOCK:, BLOCK:], pl_out[BLOCK:, BLOCK:] = li1
    ph_out[BLOCK:, 0:BLOCK], pl_out[BLOCK:, 0:BLOCK] = -b1[0], -b1[1]
    ph_out[0:BLOCK, BLOCK:] = jnp.zeros((BLOCK, BLOCK), BF16)
    pl_out[0:BLOCK, BLOCK:] = jnp.zeros((BLOCK, BLOCK), BF16)
    c0.wait()
    w[part(half, 3072), :] += r0[...]

    at1 = half + first * 768
    at2 = at1 + second * 192
    at3 = at2 + z * 24

    def out1(d):
        return push(w.at[part(half + p1[d] * 768, 768), :], r1.at[d], s1.at[d], v1.at[d], along_first(p1[d]))

    def out2(d):
        return push(w.at[part(at1 + p2[d] * 192, 192), :], r2.at[d], s2.at[d], v2.at[d], along_second(p2[d]))

    def out3(d):
        return push(w.at[part(at2 + pz[d] * 24, 24), :], r3.at[d], s3.at[d], v3.at[d], (pz[d], x, y, k))

    def whole(at, n, send, recv, peer):
        return push(full.at[part(at, n), :], full.at[part(at, n), :], send, recv, peer)

    def settle(copies):
        for copy in copies:
            copy.start()
        for copy in copies:
            copy.wait()

    settle([out1(d) for d in range(3)])
    w[part(at1, 768), :] += r1[0] + r1[1] + r1[2]
    settle([out2(d) for d in range(3)])
    w[part(at2, 192), :] += r2[0] + r2[1] + r2[2]
    settle([out3(d) for d in range(7)])
    full[part(at3, 24), :] = w[part(at3, 24), :] + ((r3[0] + r3[1]) + (r3[2] + r3[3])) + ((r3[4] + r3[5]) + r3[6])
    settle([whole(at3, 24, g3.at[d], u3.at[d], (pz[d], x, y, k)) for d in range(7)])
    settle([whole(at2, 192, g2.at[d], u2.at[d], along_second(p2[d])) for d in range(3)])
    settle([whole(at1, 768, g1.at[d], u1.at[d], along_first(p1[d])) for d in range(3)])
    settle([whole(half, 3072, g0, u0, sibling)])

    def load(block):
        return split(
            jnp.concatenate([full[pl.ds(j * 1536 + block * BLOCK, BLOCK), :] for j in range(4)], axis=1)
        )

    w11, w10, w00 = load(0), load(1), load(2)
    slab = pl.ds(pl.multiple_of(c * 64, 64), 64)
    lit1, lit0 = split(lit[1, slab, :]), split(lit[0, slab, :])
    sym1 = split(symmetric(e1 - dot3(j1, w11, 0, 0)))
    ls1 = split(dot3(lit1, sym1))
    diag_out[1] = dot3(ls1, li1)
    cross_out[...] = dot2(cg[slab, :], li0) - (dot3(split(dot3(lit1, w10)), li0) + dot3(ls1, b1))
    inner = split(dot3(w10, j0) + dot3(sym1, b2))
    cl = split(cj - dot3(li1, inner, 0, 0))
    g_zero = e0 - dot3(j0, w00, 0, 0) + dot3(b2, w10, 0, 0) - dot2(cl, xb, 0, 0)
    sym0 = split(symmetric(g_zero))
    diag_out[0] = dot3(split(dot3(lit0, sym0)), li0)


CHUNKS = 16
LINES = BLOCK // CHUNKS


def panel_kernel(
    mx, fz, fac, mf, ph, plo, grad, out,
    kept, t, arrived, yp, r0, r1, ts, tr, s0, v0, s1, v1,
):
    z, x, y, k = place()
    c = 2 * y + k
    sibling = (z, x, y, 1 - k)
    py = [lax.rem(y + d, 4) for d in (1, 2, 3)]
    before, after = lax.rem(z + 7, 8), lax.rem(z + 1, 8)
    meet([sibling] + [(z, x, p, k) for p in py] + [(before, x, y, k), (after, x, y, k)])
    lower = c <= z

    @pl.when(c == z)
    def _():
        @pl.loop(0, 16)
        def _(i):
            here = pl.ds(pl.multiple_of(i * 128, 128), 128)
            kept[here, :] = masked(mx[here, :], i * 128, x * BLOCK)

        for i in range(4):
            t[i * 128 : (i + 1) * 128, :] = dot(kept[:, i * 128 : (i + 1) * 128], fac[...], 0, 0)

    @pl.when(c < z)
    def _():
        for i in range(4):
            t[i * 128 : (i + 1) * 128, :] = dot(mx[:, i * 128 : (i + 1) * 128], fz[...], 0, 0)

    @pl.when(jnp.logical_not(lower))
    def _():
        t[...] = jnp.zeros_like(t)

    position = jnp.where(k == 0, 7 - z, (z - c + 7) & 7)
    last = z == c
    taking = (k == 1) | lower
    onward = jnp.where(k == 0, before, after)

    def chunk(i):
        here = pl.ds(i * LINES, LINES)
        return push(t.at[here, :], arrived.at[here, :], ts.at[i], tr.at[i], (onward, x, y, k))

    @pl.when(taking)
    def _():
        for i in range(CHUNKS):
            here = pl.ds(i * LINES, LINES)

            @pl.when(position > 0)
            def _():
                chunk(i).wait_recv()
                t[here, :] += arrived[here, :]

            @pl.when(jnp.logical_not(last))
            def _():
                chunk(i).start()

        @pl.when(jnp.logical_not(last))
        def _():
            for i in range(CHUNKS):
                chunk(i).wait_send()

    chip_lower = 2 * y <= z

    @pl.when(chip_lower)
    def _():
        @pl.loop(0, 4)
        def _(i):
            here = pl.ds(pl.multiple_of(i * 128, 128), 128)
            part = mf[here, :]
            part = jnp.where(last, part + t[here, :], part)
            h, l = split(part)
            for g in range(8):
                cols = slice(g * 128, (g + 1) * 128)
                start = 0 if g < 4 else BLOCK
                yp[g % 2, g // 2, here, :] = dot3(
                    (h[:, start:], l[:, start:]), (ph[start:, cols], plo[start:, cols])
                )

        swap = push(yp.at[1 - k], r0, s0, v0, sibling)
        swap.start()
        swap.wait()
        yp[pl.ds(k, 1)] += r0[...][None]
        for d in range(3):
            push(yp.at[k, py[d]], r1.at[d], s1.at[d], v1.at[d], (z, x, py[d], k)).start()

    cols = pl.ds(pl.multiple_of(c * 128, 128), 128)
    out[...] = dot2(grad[...], (ph[:, cols], plo[:, cols]))

    @pl.when(chip_lower)
    def _():
        out[...] -= yp[k, y]

    for d in range(3):
        came = lax.rem(y + 3 - d, 4)

        @pl.when(2 * came <= z)
        def _():
            push(yp.at[k, py[d]], r1.at[d], s1.at[d], v1.at[d], (z, x, py[d], k)).wait_recv()
            out[...] -= r1[d]

    @pl.when(chip_lower)
    def _():
        for d in range(3):
            push(yp.at[k, py[d]], r1.at[d], s1.at[d], v1.at[d], (z, x, py[d], k)).wait_send()


def params(number):
    return pltpu.CompilerParams(
        collective_id=number, has_side_effects=True, vmem_limit_bytes=VMEM_BYTES
    )


def shards(trail, fac, xf, lf, li, grad, cg, dg):
    dma = pltpu.SemaphoreType.DMA
    anywhere = pl.BlockSpec(memory_space=pl.ANY)
    vmem = pl.BlockSpec(memory_space=pltpu.VMEM)
    shape = jax.ShapeDtypeStruct
    mx, fz = pl.pallas_call(
        exchange_kernel,
        name="exchange",
        out_shape=(shape((2048, BLOCK), BF16), shape((2048, 1024), BF16)),
        in_specs=[anywhere] * 2,
        out_specs=[vmem, anywhere],
        scratch_shapes=[
            dma((3,)), dma((3,)), dma((2, 8)), dma((8,)), dma((2, 8)), dma((8,)), dma,
        ],
        compiler_params=params(0),
    )(trail, fac)
    cross, diag, mf, ph, plo = pl.pallas_call(
        sums_kernel,
        name="sums",
        out_shape=(
            shape((64, BLOCK), F32), shape((2, 64, BLOCK), F32), shape((BLOCK, 1024), F32),
            shape((1024, 1024), BF16), shape((1024, 1024), BF16),
        ),
        in_specs=[vmem] * 9,
        out_specs=[vmem] * 5,
        scratch_shapes=[
            pltpu.VMEM((BLOCK, 2048), BF16),
            pltpu.VMEM((6144, 128), F32),
            pltpu.VMEM((6144, 128), F32),
            pltpu.VMEM((3072, 128), F32),
            pltpu.VMEM((3, 768, 128), F32),
            pltpu.VMEM((3, 192, 128), F32),
            pltpu.VMEM((7, 24, 128), F32),
            pltpu.VMEM((2, BLOCK, BLOCK), F32),
            dma, dma, dma((3,)), dma((3,)), dma((3,)), dma((3,)), dma((7,)), dma((7,)),
            dma((7,)), dma((7,)), dma((3,)), dma((3,)), dma((3,)), dma((3,)), dma, dma,
        ],
        compiler_params=params(1),
    )(trail, fac, fz, grad, xf, lf, li, cg, dg)
    panel = pl.pallas_call(
        panel_kernel,
        name="panel",
        out_shape=shape((BLOCK, 128), F32),
        in_specs=[vmem] * 7,
        out_specs=vmem,
        scratch_shapes=[
            pltpu.VMEM((2048, BLOCK), BF16),
            pltpu.VMEM((BLOCK, 1024), F32),
            pltpu.VMEM((BLOCK, 1024), F32),
            pltpu.VMEM((2, 4, BLOCK, 128), F32),
            pltpu.VMEM((4, BLOCK, 128), F32),
            pltpu.VMEM((3, BLOCK, 128), F32),
            dma((CHUNKS,)), dma((CHUNKS,)), dma, dma, dma((3,)), dma((3,)),
        ],
        compiler_params=params(2),
    )(mx, fz, fac, mf, ph, plo, grad)
    return panel, cross, diag


def solution(mesh):
    fine = Mesh(mesh.devices.reshape(8, 4, 4, 2), ("z", "x", "y", "k"))
    row, col = ("z", "x"), ("y", "k")
    return jax.shard_map(
        shards,
        mesh=fine,
        in_specs=(P(row, col), P(col, None), P(), P(), P(), P(row, None), P(), P()),
        out_specs=(P(row, col), P(col, None), P(None, col, None)),
        check_vma=False,
    )
```

```python
import jax
import jax.numpy as jnp
from jax import lax
from jax.experimental import pallas as pl
from jax.experimental.pallas import tpu as pltpu
from jax.sharding import Mesh
from jax.sharding import PartitionSpec as P

MESH = pl.DeviceIdType.MESH
F32, BF16 = jnp.float32, jnp.bfloat16
BLOCK = 512
VMEM_BYTES = 62 * 1024 * 1024


def place():
    return tuple(lax.axis_index(a) for a in ("z", "x", "y", "k"))


def meet(peers):
    barrier = pltpu.get_barrier_semaphore()
    for peer in peers:
        pl.semaphore_signal(barrier, inc=1, device_id=peer, device_id_type=MESH)
    pl.semaphore_wait(barrier, len(peers))


def push(src, dst, send, recv, peer):
    return pltpu.make_async_remote_copy(
        src_ref=src, dst_ref=dst, send_sem=send, recv_sem=recv, device_id=peer, device_id_type=MESH
    )


def dot(a, b, ca=1, cb=0):
    return lax.dot_general(a, b, (((ca,), (cb,)), ((), ())), preferred_element_type=F32)


def split(a):
    high = a.astype(BF16)
    return high, (a - high.astype(F32)).astype(BF16)


def dot3(a, b, ca=1, cb=0):
    ah, al = a if isinstance(a, tuple) else split(a)
    bh, bl = b if isinstance(b, tuple) else split(b)
    return dot(ah, bh, ca, cb) + (dot(al, bh, ca, cb) + dot(ah, bl, ca, cb))


def dot2(a, b, ca=1, cb=0):
    if isinstance(a, tuple):
        return dot(a[0], b, ca, cb) + dot(a[1], b, ca, cb)
    return dot(a, b[0], ca, cb) + dot(a, b[1], ca, cb)


def symmetric(f):
    size = f.shape[0]
    rows = lax.broadcasted_iota(jnp.int32, (size, size), 0)
    cols = lax.broadcasted_iota(jnp.int32, (size, size), 1)
    halved = jnp.where(cols < rows, f, jnp.where(cols == rows, f * 0.5, 0.0))
    return halved + halved.T


def masked(m, row0, col0):
    rows = row0 + lax.broadcasted_iota(jnp.int32, m.shape, 0)
    cols = col0 + lax.broadcasted_iota(jnp.int32, m.shape, 1)
    scale = jnp.where(cols < rows, 1.0, jnp.where(cols == rows, 0.5, 0.0))
    return (m.astype(F32) * scale).astype(BF16)

CHUNKS = 16
LINES = BLOCK // CHUNKS
HOPS = 16


def kernel(
    trail, fac, xf, lf, li, grad, cg, dg,
    panel_out, cross_out, diag_out,
    m, fv, gv, xv, lfv, liv, cgv, dgv,
    mx, fz, f, mf, t, arrived, w, full, r1, r2, r3,
    ph, plo, pairs, consts, yp, q0, q1, tq, rt,
    ls, fs, fr, hs, hr, xs, xr,
    s0, v0, s1, v1, s2, v2, s3, v3, g3, u3, g2, u2, g1, u1, g0, u0,
    ts, tr, a0, b0, a1, b1s, es, er,
):
    z, x, y, k = place()
    c = 2 * y + k
    ys, ks = z >> 1, z & 1
    sibling = (z, x, y, 1 - k)
    lower = c <= z
    last = c == z
    chip_lower = 2 * y <= z
    source_chip = y == ys
    yn = (lax.rem(y + 3, 4), lax.rem(y + 1, 4))
    px = [lax.rem(x + d, 4) for d in (1, 2, 3)]
    py = [lax.rem(y + d, 4) for d in (1, 2, 3)]
    pz = [lax.rem(z + d, 8) for d in range(1, 8)]
    pc = [lax.rem(c + d, 8) for d in range(1, 8)]
    mine = pl.ds(pl.multiple_of(x * BLOCK, BLOCK), BLOCK)

    def local(n, src, dst):
        return pltpu.make_async_copy(src, dst, ls.at[n])

    get_trail = local(0, trail, m)
    get_factor = local(1, fac, fv)
    get_grad = local(2, grad, gv)
    get_small = [
        local(3, xf, xv), local(4, lf, lfv), local(5, li, liv), local(6, cg, cgv), local(7, dg, dgv)
    ]
    get_own = local(8, trail.at[:, mine], mx.at[mine, :])
    get_source = local(9, fac, fz)

    @pl.when(lower)
    def _():
        get_trail.start()
        get_factor.start()
        get_own.start()

    get_grad.start()
    for copy in get_small:
        copy.start()

    @pl.when(last)
    def _():
        get_source.start()

    meet(
        [(z, p, y, k) for p in px]
        + [(z, x, p >> 1, p & 1) for p in pc]
        + [(p, x, y, k) for p in pz]
    )

    def rows(s, i):
        block = lax.rem(x + i // 4, 4)
        return pl.ds(pl.multiple_of(block * BLOCK + s * 256 + lax.rem(i, 4) * 64, 64), 64)

    def first_hop(s, i):
        return push(
            fac.at[rows(s, i), :], fz.at[rows(s, i), :], fs.at[s, i], fr.at[i], (z, x, yn[s], s)
        )

    def beside_own(i):
        return push(fac.at[rows(1 - k, i), :], fz.at[rows(1 - k, i), :], hs.at[0, i], fr.at[i], sibling)

    def beside_other(i):
        return push(fac.at[rows(k, i), :], fz.at[rows(k, i), :], hs.at[1, i], hr.at[i], sibling)

    onward_y = jnp.where(k == 0, yn[0], yn[1])
    hops = jnp.where(k == 0, (ys - y + 4) & 3, (y - ys + 4) & 3)

    def forward(i):
        return push(
            fz.at[rows(k, i), :], fz.at[rows(k, i), :], fs.at[0, i], fr.at[i], (z, x, onward_y, k)
        )

    def share(i):
        return push(fz.at[rows(k, i), :], fz.at[rows(k, i), :], hs.at[0, i], hr.at[i], sibling)

    def other(i):
        return push(fz.at[rows(1 - k, i), :], fz.at[rows(1 - k, i), :], hs.at[0, i], hr.at[i], sibling)

    def across(d):
        return push(
            trail.at[:, pl.ds(pl.multiple_of(px[d] * BLOCK, 128), BLOCK)],
            mx.at[mine, :],
            xs.at[d],
            xr.at[d],
            (z, px[d], y, k),
        )

    @pl.when(last)
    def _():
        @pl.loop(0, HOPS)
        def _(i):
            first_hop(0, i).start()
            first_hop(1, i).start()
            beside_own(i).start()
            beside_other(i).start()

    @pl.when(lower)
    def _():
        for d in (2, 1, 0):
            across(d).start()

    def relays(lo, hi):
        @pl.when(jnp.logical_not(source_chip))
        def _():
            @pl.loop(lo, hi)
            def _(i):
                forward(i).wait_recv()

                @pl.when(hops < 3)
                def _():
                    forward(i).start()

                share(i).start()

        @pl.when(source_chip & (k != ks))
        def _():
            @pl.loop(lo, hi)
            def _(i):
                forward(i).wait_recv()

    def others(lo, hi):
        @pl.when(jnp.logical_not(last))
        def _():
            @pl.loop(lo, hi)
            def _(i):
                other(i).wait_recv()

    @pl.when(lower)
    def _():
        get_trail.wait()
        get_factor.wait()

        @pl.loop(0, 4)
        def _(i):
            here = pl.ds(pl.multiple_of(i * 128, 128), 128)

            @pl.when(last)
            def _():
                m[here, :] = masked(m[here, :], x * BLOCK + i * 128, 0)

            mf[here, :] = dot(m[here, :], fv[...])

    @pl.when(c > z)
    def _():
        mf[...] = jnp.zeros_like(mf)
        w[...] = jnp.zeros_like(w)
        t[...] = jnp.zeros_like(t)

    get_grad.wait()

    @pl.when(last)
    def _():
        get_source.wait()

    relays(0, 4)
    others(0, 4)

    @pl.when(lower)
    def _():
        f[...] = fz[mine, :]

    own = jnp.where(last, 1.0, 0.0)

    def add_block(block, a, b):
        @pl.when(lower)
        def _():
            mfa = mf[:, a * BLOCK : (a + 1) * BLOCK]
            mfb = mf[:, b * BLOCK : (b + 1) * BLOCK]
            ga = gv[:, a * BLOCK : (a + 1) * BLOCK].astype(F32) * own
            fa = f[:, a * BLOCK : (a + 1) * BLOCK]
            fb = f[:, b * BLOCK : (b + 1) * BLOCK]
            value = dot2(split(ga - mfa), fb, 0, 0) - dot2(fa, split(mfb), 0, 0)
            for j in range(4):
                w[pl.ds(j * 1536 + block * BLOCK, BLOCK), :] = value[:, j * 128 : (j + 1) * 128]

    add_block(0, 1, 1)
    relays(4, 6)
    add_block(1, 1, 0)
    relays(6, 8)
    add_block(2, 0, 0)

    half = k * 3072
    first = jnp.where(k == 0, y, x)
    second = jnp.where(k == 0, x, y)
    p1 = [lax.rem(first + d, 4) for d in (1, 2, 3)]
    p2 = [lax.rem(second + d, 4) for d in (1, 2, 3)]
    at1 = half + first * 768
    at2 = at1 + second * 192
    at3 = at2 + z * 24

    def part(at, n):
        return pl.ds(pl.multiple_of(at, 8), n)

    def along_first(p):
        return (z, jnp.where(k == 0, x, p), jnp.where(k == 0, p, y), k)

    def along_second(p):
        return (z, jnp.where(k == 0, p, x), jnp.where(k == 0, y, p), k)

    def out1(d):
        return push(w.at[part(half + p1[d] * 768, 768), :], r1.at[d], s1.at[d], v1.at[d], along_first(p1[d]))

    def out2(d):
        return push(w.at[part(at1 + p2[d] * 192, 192), :], r2.at[d], s2.at[d], v2.at[d], along_second(p2[d]))

    def out3(d):
        return push(w.at[part(at2 + pz[d] * 24, 24), :], r3.at[d], s3.at[d], v3.at[d], (pz[d], x, y, k))

    def whole(at, n, send, recv, peer):
        return push(full.at[part(at, n), :], full.at[part(at, n), :], send, recv, peer)

    def start(copies):
        for copy in copies:
            copy.start()

    def finish(copies):
        for copy in copies:
            copy.wait()

    other_half = part(3072 - half, 3072)
    c0 = [push(w.at[other_half, :], full.at[other_half, :], s0, v0, sibling)]
    c1 = [out1(d) for d in range(3)]
    c2 = [out2(d) for d in range(3)]
    c3 = [out3(d) for d in range(7)]
    c4 = [whole(at3, 24, g3.at[d], u3.at[d], (pz[d], x, y, k)) for d in range(7)]
    c5 = [whole(at2, 192, g2.at[d], u2.at[d], along_second(p2[d])) for d in range(3)]
    c6 = [whole(at1, 768, g1.at[d], u1.at[d], along_first(p1[d])) for d in range(3)]
    c7 = [whole(half, 3072, g0, u0, sibling)]
    start(c0)

    def pre_one():
        finish(get_small)
        li0, li1 = split(liv[0]), split(liv[1])
        ph[0:BLOCK, 0:BLOCK], plo[0:BLOCK, 0:BLOCK] = li0
        ph[BLOCK:, BLOCK:], plo[BLOCK:, BLOCK:] = li1
        ph[0:BLOCK, BLOCK:] = jnp.zeros((BLOCK, BLOCK), BF16)
        plo[0:BLOCK, BLOCK:] = jnp.zeros((BLOCK, BLOCK), BF16)
        high, low = split(dot3(split(dot2(li1, xv[...])), li0))
        ph[BLOCK:, 0:BLOCK], plo[BLOCK:, 0:BLOCK] = -high, -low

    def li0():
        return ph[0:BLOCK, 0:BLOCK], plo[0:BLOCK, 0:BLOCK]

    def li1():
        return ph[BLOCK:, BLOCK:], plo[BLOCK:, BLOCK:]

    def minus_b1():
        return ph[BLOCK:, 0:BLOCK], plo[BLOCK:, 0:BLOCK]

    def pair(n):
        return pairs[2 * n], pairs[2 * n + 1]

    def keep(n, value):
        pairs[2 * n], pairs[2 * n + 1] = split(value)

    def pre_two():
        keep(0, dot2(li0(), lfv[0]))
        keep(1, dot2(li1(), lfv[1]))
        keep(2, -dot2(minus_b1(), lfv[0]))

    def pre_three():
        consts[0] = dot(lfv[0], dgv[0], 0, 0)
        consts[1] = dot(lfv[1], dgv[1], 0, 0)
        consts[2] = dot2(cgv[...], pair(0))

    def transposed(j):
        @pl.when(lower)
        def _():
            if j == 0:
                get_own.wait()
            else:
                across(3 - j).wait_recv()
            block = lax.rem(x + j, 4)
            here = pl.ds(pl.multiple_of(block * BLOCK, BLOCK), BLOCK)

            @pl.when(last)
            def _():
                mx[here, :] = masked(mx[here, :], block * BLOCK, x * BLOCK)

            @pl.loop(0, 4)
            def _(i):
                lines = pl.ds(pl.multiple_of(i * 128, 128), 128)
                value = dot(mx[here, lines], fz[here, :], 0, 0)
                if j == 0:
                    t[lines, :] = value
                else:
                    t[lines, :] += value

    pre_one()
    relays(8, 9)
    transposed(0)
    relays(9, 10)
    pre_two()
    relays(10, 11)
    finish(c0)
    w[part(half, 3072), :] += full[part(half, 3072), :]
    start(c1)
    relays(11, 12)
    others(4, 8)
    transposed(1)
    relays(12, 14)
    others(8, 12)
    transposed(2)
    relays(14, 16)
    others(12, 16)
    transposed(3)

    before, after = lax.rem(z + 7, 8), lax.rem(z + 1, 8)
    position = jnp.where(k == 0, 7 - z, (z - c + 7) & 7)
    taking = (k == 1) | lower
    onward_z = jnp.where(k == 0, before, after)

    def chunk(i):
        here = pl.ds(i * LINES, LINES)
        return push(t.at[here, :], arrived.at[here, :], ts.at[i], tr.at[i], (onward_z, x, y, k))

    def chain(i):
        here = pl.ds(i * LINES, LINES)

        @pl.when(taking)
        def _():
            @pl.when(position > 0)
            def _():
                chunk(i).wait_recv()
                t[here, :] += arrived[here, :]

            @pl.when(jnp.logical_not(last))
            def _():
                chunk(i).start()

    def mapped(part_rows, store):
        h, l = split(part_rows)
        for g in range(8):
            cols = slice(g * 128, (g + 1) * 128)
            at = 0 if g < 4 else BLOCK
            store(g, dot3((h[:, at:], l[:, at:]), (ph[at:, cols], plo[at:, cols])))

    def direct(i):
        @pl.when(chip_lower)
        def _():
            here = slice(i * 128, (i + 1) * 128)

            def store(g, value):
                yp[g % 2, g // 2, here, :] = value

            mapped(mf[here, :], store)

    swap = push(yp.at[1 - k], q0, a0, b0, sibling)

    def spread(d):
        return push(yp.at[k, py[d]], q1.at[d], a1.at[d], b1s.at[d], (z, x, py[d], k))

    def swap_start():
        @pl.when(chip_lower)
        def _():
            swap.start()

    def swap_end():
        @pl.when(chip_lower)
        def _():
            swap.wait()
            yp[pl.ds(k, 1)] += q0[...][None]
            for d in range(3):
                spread(d).start()

    def scatter(d, i):
        here = pl.ds(i * 128, 128)
        to = pc[d]
        return push(tq.at[to, here, :], rt.at[here, :], es.at[d, i], er.at[i], (z, x, to >> 1, to & 1))

    def last_part(i):
        @pl.when(last)
        def _():
            here = slice(i * 128, (i + 1) * 128)

            def store(g, value):
                tq[g, here, :] = value

            mapped(t[here, :], store)
            for d in range(7):
                scatter(d, i).start()

    def sum_one():
        finish(c1)
        w[part(at1, 768), :] += r1[0] + r1[1] + r1[2]
        start(c2)

    def sum_two():
        finish(c2)
        w[part(at2, 192), :] += r2[0] + r2[1] + r2[2]
        start(c3)

    def sum_three():
        finish(c3)
        full[part(at3, 24), :] = w[part(at3, 24), :] + (
            ((r3[0] + r3[1]) + (r3[2] + r3[3])) + ((r3[4] + r3[5]) + r3[6])
        )
        start(c4)

    def then(done, go):
        def run():
            finish(done)
            start(go)

        return run

    beside = {
        0: [sum_one],
        1: [lambda: direct(0)],
        2: [sum_two],
        3: [lambda: direct(1)],
        4: [sum_three],
        5: [lambda: direct(2)],
        6: [then(c4, c5)],
        7: [lambda: direct(3), swap_start],
        8: [then(c5, c6)],
        9: [swap_end],
        10: [pre_three],
        11: [then(c6, c7)],
    }
    for i in range(CHUNKS):
        chain(i)
        if i % 4 == 3:
            last_part(i // 4)
        for step in beside.get(i, []):
            step()

    finish(c7)

    def load(block):
        return split(
            jnp.concatenate([full[pl.ds(j * 1536 + block * BLOCK, BLOCK), :] for j in range(4)], axis=1)
        )

    w11, w10, w00 = load(0), load(1), load(2)
    slab = pl.ds(pl.multiple_of(c * 64, 64), 64)
    pick = jnp.where(
        lax.broadcasted_iota(jnp.int32, (BLOCK, 64), 0)
        == c * 64 + lax.broadcasted_iota(jnp.int32, (BLOCK, 64), 1),
        1.0,
        0.0,
    ).astype(BF16)

    def turned(parts):
        return tuple(dot(pick, part_of, 0, 1).astype(BF16) for part_of in parts)

    lit1, lit0 = turned(li1()), turned(li0())
    sym1 = split(symmetric(consts[1] - dot3(pair(1), w11, 0, 0)))
    inner = split(dot3(w10, pair(0)) + dot3(sym1, pair(2)))
    cl = split(consts[2] - dot3(li1(), inner, 0, 0))
    g_zero = consts[0] - dot3(pair(0), w00, 0, 0) + dot3(pair(2), w10, 0, 0) - dot2(cl, xv[...], 0, 0)
    sym0 = split(symmetric(g_zero))
    ls1 = split(dot3(lit1, sym1))
    diag_out[1] = dot3(ls1, li1())
    cross_out[...] = dot2(cgv[slab, :], li0()) - (
        dot3(split(dot3(lit1, w10)), li0()) - dot3(ls1, minus_b1())
    )
    diag_out[0] = dot3(split(dot3(lit0, sym0)), li0())

    cols = pl.ds(pl.multiple_of(c * 128, 128), 128)
    panel_out[...] = dot2(gv[...], (ph[:, cols], plo[:, cols]))

    @pl.when(chip_lower)
    def _():
        panel_out[...] -= yp[k, y]

    for d in range(3):
        @pl.when(2 * lax.rem(y + 3 - d, 4) <= z)
        def _():
            spread(d).wait_recv()
            panel_out[...] -= q1[d]

    @pl.when(last)
    def _():
        panel_out[...] -= tq[c]

    @pl.when(jnp.logical_not(last))
    def _():
        for i in range(4):
            scatter(0, i).wait_recv()
        panel_out[...] -= rt[...]

    @pl.when(last)
    def _():
        @pl.loop(0, HOPS)
        def _(i):
            first_hop(0, i).wait_send()
            first_hop(1, i).wait_send()
            beside_own(i).wait_send()
            beside_other(i).wait_send()

        for i in range(4):
            for d in range(7):
                scatter(d, i).wait_send()

    @pl.when(jnp.logical_not(source_chip))
    def _():
        @pl.loop(0, HOPS)
        def _(i):
            share(i).wait_send()

            @pl.when(hops < 3)
            def _():
                forward(i).wait_send()

    @pl.when(lower)
    def _():
        for d in range(3):
            across(d).wait_send()

    @pl.when(taking & jnp.logical_not(last))
    def _():
        for i in range(CHUNKS):
            chunk(i).wait_send()

    @pl.when(chip_lower)
    def _():
        for d in range(3):
            spread(d).wait_send()


def shards(trail, fac, xf, lf, li, grad, cg, dg):
    dma = pltpu.SemaphoreType.DMA
    anywhere = pl.BlockSpec(memory_space=pl.ANY)
    vmem = pl.BlockSpec(memory_space=pltpu.VMEM)
    shape = jax.ShapeDtypeStruct
    square = (BLOCK, BLOCK)
    return pl.pallas_call(
        kernel,
        name="adjoint",
        out_shape=(
            shape((BLOCK, 128), F32), shape((64, BLOCK), F32), shape((2, 64, BLOCK), F32),
        ),
        in_specs=[anywhere] * 8,
        out_specs=[vmem] * 3,
        scratch_shapes=[
            pltpu.VMEM((BLOCK, 2048), BF16),
            pltpu.VMEM((2048, 1024), BF16),
            pltpu.VMEM((BLOCK, 1024), BF16),
            pltpu.VMEM(square, BF16),
            pltpu.VMEM((2, *square), BF16),
            pltpu.VMEM((2, *square), F32),
            pltpu.VMEM(square, BF16),
            pltpu.VMEM((2, *square), BF16),
            pltpu.VMEM((2048, BLOCK), BF16),
            pltpu.VMEM((2048, 1024), BF16),
            pltpu.VMEM((BLOCK, 1024), BF16),
            pltpu.VMEM((BLOCK, 1024), F32),
            pltpu.VMEM((BLOCK, 1024), F32),
            pltpu.VMEM((BLOCK, 1024), F32),
            pltpu.VMEM((6144, 128), F32),
            pltpu.VMEM((6144, 128), F32),
            pltpu.VMEM((3, 768, 128), F32),
            pltpu.VMEM((3, 192, 128), F32),
            pltpu.VMEM((7, 24, 128), F32),
            pltpu.VMEM((1024, 1024), BF16),
            pltpu.VMEM((1024, 1024), BF16),
            pltpu.VMEM((6, *square), BF16),
            pltpu.VMEM((3, *square), F32),
            pltpu.VMEM((2, 4, BLOCK, 128), F32),
            pltpu.VMEM((4, BLOCK, 128), F32),
            pltpu.VMEM((3, BLOCK, 128), F32),
            pltpu.VMEM((8, BLOCK, 128), F32),
            pltpu.VMEM((BLOCK, 128), F32),
            dma((10,)), dma((2, HOPS)), dma((HOPS,)), dma((2, HOPS)), dma((HOPS,)), dma((3,)), dma((3,)),
            dma, dma, dma((3,)), dma((3,)), dma((3,)), dma((3,)), dma((7,)), dma((7,)),
            dma((7,)), dma((7,)), dma((3,)), dma((3,)), dma((3,)), dma((3,)), dma, dma,
            dma((CHUNKS,)), dma((CHUNKS,)), dma, dma, dma((3,)), dma((3,)), dma((7, 4)), dma((4,)),
        ],
        compiler_params=pltpu.CompilerParams(
            collective_id=0, has_side_effects=True, vmem_limit_bytes=VMEM_BYTES
        ),
    )(trail, fac, xf, lf, li, grad, cg, dg)


def solution(mesh):
    fine = Mesh(mesh.devices.reshape(8, 4, 4, 2), ("z", "x", "y", "k"))
    row, col = ("z", "x"), ("y", "k")
    return jax.shard_map(
        shards,
        mesh=fine,
        in_specs=(P(row, col), P(col, None), P(), P(), P(), P(row, None), P(), P()),
        out_specs=(P(row, col), P(col, None), P(None, col, None)),
        check_vma=False,
    )
```

```python
import jax
import jax.numpy as jnp
from jax import lax
from jax.experimental import pallas as pl
from jax.experimental.pallas import tpu as pltpu
from jax.sharding import Mesh
from jax.sharding import PartitionSpec as P

MESH = pl.DeviceIdType.MESH
F32, BF16 = jnp.float32, jnp.bfloat16
BLOCK = 512
VMEM_BYTES = 62 * 1024 * 1024


def place():
    return tuple(lax.axis_index(a) for a in ("z", "x", "y", "k"))


def meet(peers):
    barrier = pltpu.get_barrier_semaphore()
    for peer in peers:
        pl.semaphore_signal(barrier, inc=1, device_id=peer, device_id_type=MESH)
    pl.semaphore_wait(barrier, len(peers))


def push(src, dst, send, recv, peer):
    return pltpu.make_async_remote_copy(
        src_ref=src, dst_ref=dst, send_sem=send, recv_sem=recv, device_id=peer, device_id_type=MESH
    )


def dot(a, b, ca=1, cb=0):
    return lax.dot_general(a, b, (((ca,), (cb,)), ((), ())), preferred_element_type=F32)


def split(a):
    high = a.astype(BF16)
    return high, (a - high.astype(F32)).astype(BF16)


def dot3(a, b, ca=1, cb=0):
    ah, al = a if isinstance(a, tuple) else split(a)
    bh, bl = b if isinstance(b, tuple) else split(b)
    return dot(ah, bh, ca, cb) + (dot(al, bh, ca, cb) + dot(ah, bl, ca, cb))


def dot2(a, b, ca=1, cb=0):
    if isinstance(a, tuple):
        return dot(a[0], b, ca, cb) + dot(a[1], b, ca, cb)
    return dot(a, b[0], ca, cb) + dot(a, b[1], ca, cb)


def symmetric(f):
    size = f.shape[0]
    rows = lax.broadcasted_iota(jnp.int32, (size, size), 0)
    cols = lax.broadcasted_iota(jnp.int32, (size, size), 1)
    halved = jnp.where(cols < rows, f, jnp.where(cols == rows, f * 0.5, 0.0))
    return halved + halved.T


def masked(m, row0, col0):
    rows = row0 + lax.broadcasted_iota(jnp.int32, m.shape, 0)
    cols = col0 + lax.broadcasted_iota(jnp.int32, m.shape, 1)
    scale = jnp.where(cols < rows, 1.0, jnp.where(cols == rows, 0.5, 0.0))
    return (m.astype(F32) * scale).astype(BF16)

CHUNKS = 16
LINES = BLOCK // CHUNKS
HOPS = 16


def kernel(
    trail, fac, xf, lf, li, grad, cg, dg,
    panel_out, cross_out, diag_out,
    m, fv, gv, xv, lfv, liv, cgv, dgv,
    mx, fz, f, mf, t, arrived, w, full, r1, r2, r3,
    ph, plo, pairs, consts, yp, q0, q1, tq, rt,
    ls, fs, fr, hs, hr, xs, xr,
    s0, v0, s1, v1, s2, v2, s3, v3, g3, u3, g2, u2, g1, u1, g0, u0,
    ts, tr, a0, b0, a1, b1s, es, er,
):
    z, x, y, k = place()
    c = 2 * y + k
    ys, ks = z >> 1, z & 1
    sibling = (z, x, y, 1 - k)
    lower = c <= z
    last = c == z
    chip_lower = 2 * y <= z
    source_chip = y == ys
    yn = (lax.rem(y + 3, 4), lax.rem(y + 1, 4))
    px = [lax.rem(x + d, 4) for d in (1, 2, 3)]
    py = [lax.rem(y + d, 4) for d in (1, 2, 3)]
    pz = [lax.rem(z + d, 8) for d in range(1, 8)]
    pc = [lax.rem(c + d, 8) for d in range(1, 8)]
    mine = pl.ds(pl.multiple_of(x * BLOCK, BLOCK), BLOCK)

    def local(n, src, dst):
        return pltpu.make_async_copy(src, dst, ls.at[n])

    get_trail = local(0, trail, m)
    get_factor = local(1, fac, fv)
    get_grad = local(2, grad, gv)
    get_small = [
        local(3, xf, xv), local(4, lf, lfv), local(5, li, liv), local(6, cg, cgv), local(7, dg, dgv)
    ]
    get_own = local(8, trail.at[:, mine], mx.at[mine, :])
    get_source = local(9, fac, fz)

    @pl.when(lower)
    def _():
        get_trail.start()
        get_factor.start()
        get_own.start()

    get_grad.start()
    for copy in get_small:
        copy.start()

    @pl.when(last)
    def _():
        get_source.start()

    meet(
        [(z, p, y, k) for p in px]
        + [(z, x, p >> 1, p & 1) for p in pc]
        + [(p, x, y, k) for p in pz]
    )

    def rows(s, i):
        block = lax.rem(x + i // 4, 4)
        return pl.ds(pl.multiple_of(block * BLOCK + s * 256 + lax.rem(i, 4) * 64, 64), 64)

    def first_hop(s, i):
        return push(
            fac.at[rows(s, i), :], fz.at[rows(s, i), :], fs.at[s, i], fr.at[i], (z, x, yn[s], s)
        )

    def beside_own(i):
        return push(fac.at[rows(1 - k, i), :], fz.at[rows(1 - k, i), :], hs.at[0, i], fr.at[i], sibling)

    def beside_other(i):
        return push(fac.at[rows(k, i), :], fz.at[rows(k, i), :], hs.at[1, i], hr.at[i], sibling)

    onward_y = jnp.where(k == 0, yn[0], yn[1])
    hops = jnp.where(k == 0, (ys - y + 4) & 3, (y - ys + 4) & 3)

    def forward(i):
        return push(
            fz.at[rows(k, i), :], fz.at[rows(k, i), :], fs.at[0, i], fr.at[i], (z, x, onward_y, k)
        )

    def share(i):
        return push(fz.at[rows(k, i), :], fz.at[rows(k, i), :], hs.at[0, i], hr.at[i], sibling)

    def other(i):
        return push(fz.at[rows(1 - k, i), :], fz.at[rows(1 - k, i), :], hs.at[0, i], hr.at[i], sibling)

    def across(d):
        return push(
            trail.at[:, pl.ds(pl.multiple_of(px[d] * BLOCK, 128), BLOCK)],
            mx.at[mine, :],
            xs.at[d],
            xr.at[d],
            (z, px[d], y, k),
        )

    def feed(lo, hi):
        @pl.when(last)
        def _():
            @pl.loop(lo, min(hi, HOPS))
            def _(i):
                @pl.when(i >= 2)
                def _():
                    first_hop(0, i - 2).wait_send()
                    first_hop(1, i - 2).wait_send()

                first_hop(0, i).start()
                first_hop(1, i).start()
                beside_own(i).start()
                beside_other(i).start()

    feed(0, 2)

    @pl.when(lower)
    def _():
        for d in (2, 1, 0):
            across(d).start()

    def relays(lo, hi):
        feed(lo + 2, hi + 2)

        @pl.when(jnp.logical_not(source_chip))
        def _():
            @pl.loop(lo, hi)
            def _(i):
                forward(i).wait_recv()

                @pl.when(hops < 3)
                def _():
                    forward(i).start()

                share(i).start()

        @pl.when(source_chip & (k != ks))
        def _():
            @pl.loop(lo, hi)
            def _(i):
                forward(i).wait_recv()

    def others(lo, hi):
        @pl.when(jnp.logical_not(last))
        def _():
            @pl.loop(lo, hi)
            def _(i):
                other(i).wait_recv()

    @pl.when(lower)
    def _():
        get_trail.wait()
        get_factor.wait()

        @pl.loop(0, 4)
        def _(i):
            here = pl.ds(pl.multiple_of(i * 128, 128), 128)

            @pl.when(last)
            def _():
                m[here, :] = masked(m[here, :], x * BLOCK + i * 128, 0)

            mf[here, :] = dot(m[here, :], fv[...])

    @pl.when(c > z)
    def _():
        mf[...] = jnp.zeros_like(mf)
        w[...] = jnp.zeros_like(w)
        t[...] = jnp.zeros_like(t)

    get_grad.wait()

    @pl.when(last)
    def _():
        get_source.wait()

    relays(0, 4)
    others(0, 4)

    @pl.when(lower)
    def _():
        f[...] = fz[mine, :]

    own = jnp.where(last, 1.0, 0.0)

    def add_block(block, a, b):
        @pl.when(lower)
        def _():
            mfa = mf[:, a * BLOCK : (a + 1) * BLOCK]
            mfb = mf[:, b * BLOCK : (b + 1) * BLOCK]
            ga = gv[:, a * BLOCK : (a + 1) * BLOCK].astype(F32) * own
            fa = f[:, a * BLOCK : (a + 1) * BLOCK]
            fb = f[:, b * BLOCK : (b + 1) * BLOCK]
            value = dot2(split(ga - mfa), fb, 0, 0) - dot2(fa, split(mfb), 0, 0)
            for j in range(4):
                w[pl.ds(j * 1536 + block * BLOCK, BLOCK), :] = value[:, j * 128 : (j + 1) * 128]

    add_block(0, 1, 1)
    relays(4, 6)
    add_block(1, 1, 0)
    relays(6, 8)
    add_block(2, 0, 0)

    half = k * 3072
    first = jnp.where(k == 0, y, x)
    second = jnp.where(k == 0, x, y)
    p1 = [lax.rem(first + d, 4) for d in (1, 2, 3)]
    p2 = [lax.rem(second + d, 4) for d in (1, 2, 3)]
    at1 = half + first * 768
    at2 = at1 + second * 192
    at3 = at2 + z * 24

    def part(at, n):
        return pl.ds(pl.multiple_of(at, 8), n)

    def along_first(p):
        return (z, jnp.where(k == 0, x, p), jnp.where(k == 0, p, y), k)

    def along_second(p):
        return (z, jnp.where(k == 0, p, x), jnp.where(k == 0, y, p), k)

    def out1(d):
        return push(w.at[part(half + p1[d] * 768, 768), :], r1.at[d], s1.at[d], v1.at[d], along_first(p1[d]))

    def out2(d):
        return push(w.at[part(at1 + p2[d] * 192, 192), :], r2.at[d], s2.at[d], v2.at[d], along_second(p2[d]))

    def out3(d):
        return push(w.at[part(at2 + pz[d] * 24, 24), :], r3.at[d], s3.at[d], v3.at[d], (pz[d], x, y, k))

    def whole(at, n, send, recv, peer):
        return push(full.at[part(at, n), :], full.at[part(at, n), :], send, recv, peer)

    def start(copies):
        for copy in copies:
            copy.start()

    def finish(copies):
        for copy in copies:
            copy.wait()

    def quarter(at, j):
        return part(at + lax.rem(j, 4) * 768, 768)

    def swapped(j):
        away = quarter(3072 - half, second + 1 + j)
        return push(w.at[away, :], full.at[away, :], s0.at[j], v0.at[j], sibling)

    c0 = [swapped(j) for j in range(4)]
    c1 = [out1(d) for d in range(3)]
    c2 = [out2(d) for d in range(3)]
    c3 = [out3(d) for d in range(7)]
    c4 = [whole(at3, 24, g3.at[d], u3.at[d], (pz[d], x, y, k)) for d in range(7)]
    c5 = [whole(at2, 192, g2.at[d], u2.at[d], along_second(p2[d])) for d in range(3)]
    c6 = [whole(at1, 768, g1.at[d], u1.at[d], along_first(p1[d])) for d in range(3)]
    c7 = [
        whole(half + lax.rem(first + 4 - j, 4) * 768, 768, g0.at[j], u0.at[j], sibling) for j in range(4)
    ]
    start(c0)

    def pre_one():
        finish(get_small)
        li0, li1 = split(liv[0]), split(liv[1])
        ph[0:BLOCK, 0:BLOCK], plo[0:BLOCK, 0:BLOCK] = li0
        ph[BLOCK:, BLOCK:], plo[BLOCK:, BLOCK:] = li1
        ph[0:BLOCK, BLOCK:] = jnp.zeros((BLOCK, BLOCK), BF16)
        plo[0:BLOCK, BLOCK:] = jnp.zeros((BLOCK, BLOCK), BF16)
        high, low = split(dot3(split(dot2(li1, xv[...])), li0))
        ph[BLOCK:, 0:BLOCK], plo[BLOCK:, 0:BLOCK] = -high, -low

    def li0():
        return ph[0:BLOCK, 0:BLOCK], plo[0:BLOCK, 0:BLOCK]

    def li1():
        return ph[BLOCK:, BLOCK:], plo[BLOCK:, BLOCK:]

    def minus_b1():
        return ph[BLOCK:, 0:BLOCK], plo[BLOCK:, 0:BLOCK]

    def pair(n):
        return pairs[2 * n], pairs[2 * n + 1]

    def keep(n, value):
        pairs[2 * n], pairs[2 * n + 1] = split(value)

    def pre_two():
        keep(0, dot2(li0(), lfv[0]))
        keep(1, dot2(li1(), lfv[1]))
        keep(2, -dot2(minus_b1(), lfv[0]))

    def pre_three():
        consts[0] = dot(lfv[0], dgv[0], 0, 0)
        consts[1] = dot(lfv[1], dgv[1], 0, 0)
        consts[2] = dot2(cgv[...], pair(0))

    def transposed(j):
        @pl.when(lower)
        def _():
            if j == 0:
                get_own.wait()
            else:
                across(3 - j).wait_recv()
            block = lax.rem(x + j, 4)
            here = pl.ds(pl.multiple_of(block * BLOCK, BLOCK), BLOCK)

            @pl.when(last)
            def _():
                mx[here, :] = masked(mx[here, :], block * BLOCK, x * BLOCK)

            @pl.loop(0, 2)
            def _(i):
                lines = pl.ds(pl.multiple_of(i * 256, 256), 256)
                value = dot(mx[here, lines], fz[here, :], 0, 0)
                if j == 0:
                    t[lines, :] = value
                else:
                    t[lines, :] += value

    pre_one()
    relays(8, 9)
    transposed(0)
    relays(9, 10)
    pre_two()
    relays(10, 11)
    for j in range(4):
        c0[j].wait_recv()
        here = quarter(half, first + 1 + j)
        w[here, :] += full[here, :]
        if j < 3:
            c1[j].start()
    relays(11, 12)
    others(4, 8)
    transposed(1)
    relays(12, 14)
    others(8, 12)
    transposed(2)
    relays(14, 16)
    others(12, 16)
    transposed(3)

    before, after = lax.rem(z + 7, 8), lax.rem(z + 1, 8)
    position = jnp.where(k == 0, 7 - z, (z - c + 7) & 7)
    taking = (k == 1) | lower
    onward_z = jnp.where(k == 0, before, after)

    def chunk(i):
        here = pl.ds(pl.multiple_of(i * LINES, LINES), LINES)
        return push(t.at[here, :], arrived.at[here, :], ts.at[i], tr.at[i], (onward_z, x, y, k))

    def mapped(part_rows, store):
        h, l = split(part_rows)
        low = dot3((h, l), (ph[:, :BLOCK], plo[:, :BLOCK]))
        high = dot3((h[:, BLOCK:], l[:, BLOCK:]), (ph[BLOCK:, BLOCK:], plo[BLOCK:, BLOCK:]))
        for g in range(4):
            store(g, low[:, g * 128 : (g + 1) * 128])
            store(g + 4, high[:, g * 128 : (g + 1) * 128])

    def direct(i):
        @pl.when(chip_lower)
        def _():
            here = slice(i * 128, (i + 1) * 128)

            def store(g, value):
                yp[g % 2, g // 2, here, :] = value

            mapped(mf[here, :], store)

    swap = push(yp.at[1 - k], q0, a0, b0, sibling)

    def spread(d):
        return push(yp.at[k, py[d]], q1.at[d], a1.at[d], b1s.at[d], (z, x, py[d], k))

    def swap_start():
        @pl.when(chip_lower)
        def _():
            swap.start()

    def swap_end():
        @pl.when(chip_lower)
        def _():
            swap.wait()
            yp[pl.ds(k, 1)] += q0[...][None]
            for d in range(3):
                spread(d).start()

    def scatter(d, i):
        here = pl.ds(pl.multiple_of(i * 128, 128), 128)
        to = pc[d]
        return push(tq.at[to, here, :], rt.at[here, :], es.at[d, i], er.at[i], (z, x, to >> 1, to & 1))

    def last_part(i):
        here = pl.ds(pl.multiple_of(i * 128, 128), 128)

        def store(g, value):
            tq[g, here, :] = value

        mapped(t[here, :], store)
        for d in range(7):
            scatter(d, i).start()

    def chain(s):
        i = s - 2 * position

        @pl.when(taking & (i >= 0) & (i < CHUNKS))
        def _():
            here = pl.ds(pl.multiple_of(i * LINES, LINES), LINES)

            @pl.when(position > 0)
            def _():
                chunk(i).wait_recv()
                t[here, :] += arrived[here, :]

            @pl.when(jnp.logical_not(last))
            def _():
                @pl.when(i >= 2)
                def _():
                    chunk(i - 2).wait_send()

                chunk(i).start()

            @pl.when(last & (lax.rem(i, 4) == 3))
            def _():
                last_part(i >> 2)

    def sum_one():
        finish(c1)
        w[part(at1, 768), :] += r1[0] + r1[1] + r1[2]
        start(c2)

    def sum_two():
        finish(c2)
        w[part(at2, 192), :] += r2[0] + r2[1] + r2[2]
        start(c3)

    def sum_three():
        finish(c3)
        full[part(at3, 24), :] = w[part(at3, 24), :] + (
            ((r3[0] + r3[1]) + (r3[2] + r3[3])) + ((r3[4] + r3[5]) + r3[6])
        )
        start(c4)

    def then(done, go):
        def run():
            finish(done)
            start(go)

        return run

    def gather_one():
        finish(c5)
        start(c6)
        c7[0].start()

    def gather_two():
        for d in range(3):
            c6[d].wait_recv()
            c7[d + 1].start()

    beside = {
        1: lambda: direct(0),
        3: sum_one,
        4: lambda: direct(1),
        6: sum_two,
        7: lambda: direct(2),
        9: sum_three,
        10: lambda: direct(3),
        11: swap_start,
        12: then(c4, c5),
        13: pre_three,
        15: gather_one,
        17: swap_end,
        21: gather_two,
    }

    @pl.loop(0, CHUNKS + 14)
    def _(s):
        chain(s)
        for at, step in beside.items():
            pl.when(s == at)(step)

    for copy in c0 + c6:
        copy.wait_send()
    finish(c7)

    def load(block):
        return split(
            jnp.concatenate([full[pl.ds(j * 1536 + block * BLOCK, BLOCK), :] for j in range(4)], axis=1)
        )

    w11, w10, w00 = load(0), load(1), load(2)
    slab = pl.ds(pl.multiple_of(c * 64, 64), 64)
    pick = jnp.where(
        lax.broadcasted_iota(jnp.int32, (BLOCK, 64), 0)
        == c * 64 + lax.broadcasted_iota(jnp.int32, (BLOCK, 64), 1),
        1.0,
        0.0,
    ).astype(BF16)

    def turned(parts):
        return tuple(dot(pick, part_of, 0, 1).astype(BF16) for part_of in parts)

    lit1, lit0 = turned(li1()), turned(li0())
    sym1 = split(symmetric(consts[1] - dot3(pair(1), w11, 0, 0)))
    inner = split(dot3(w10, pair(0)) + dot3(sym1, pair(2)))
    cl = split(consts[2] - dot3(li1(), inner, 0, 0))
    g_zero = consts[0] - dot3(pair(0), w00, 0, 0) + dot3(pair(2), w10, 0, 0) - dot2(cl, xv[...], 0, 0)
    sym0 = split(symmetric(g_zero))
    ls1 = split(dot3(lit1, sym1))
    diag_out[1] = dot3(ls1, li1())
    cross_out[...] = dot2(cgv[slab, :], li0()) - (
        dot3(split(dot3(lit1, w10)), li0()) - dot3(ls1, minus_b1())
    )
    diag_out[0] = dot3(split(dot3(lit0, sym0)), li0())

    cols = pl.ds(pl.multiple_of(c * 128, 128), 128)
    panel_out[...] = dot2(gv[...], (ph[:, cols], plo[:, cols]))

    @pl.when(chip_lower)
    def _():
        panel_out[...] -= yp[k, y]

    for d in range(3):
        @pl.when(2 * lax.rem(y + 3 - d, 4) <= z)
        def _():
            spread(d).wait_recv()
            panel_out[...] -= q1[d]

    @pl.when(last)
    def _():
        panel_out[...] -= tq[c]

    @pl.when(jnp.logical_not(last))
    def _():
        for i in range(4):
            scatter(0, i).wait_recv()
        panel_out[...] -= rt[...]

    @pl.when(last)
    def _():
        @pl.loop(0, HOPS)
        def _(i):
            beside_own(i).wait_send()
            beside_other(i).wait_send()

        for i in (HOPS - 2, HOPS - 1):
            first_hop(0, i).wait_send()
            first_hop(1, i).wait_send()

        for i in range(4):
            for d in range(7):
                scatter(d, i).wait_send()

    @pl.when(jnp.logical_not(source_chip))
    def _():
        @pl.loop(0, HOPS)
        def _(i):
            share(i).wait_send()

            @pl.when(hops < 3)
            def _():
                forward(i).wait_send()

    @pl.when(lower)
    def _():
        for d in range(3):
            across(d).wait_send()

    @pl.when(taking & jnp.logical_not(last))
    def _():
        for i in (CHUNKS - 2, CHUNKS - 1):
            chunk(i).wait_send()

    @pl.when(chip_lower)
    def _():
        for d in range(3):
            spread(d).wait_send()


def shards(trail, fac, xf, lf, li, grad, cg, dg):
    dma = pltpu.SemaphoreType.DMA
    anywhere = pl.BlockSpec(memory_space=pl.ANY)
    vmem = pl.BlockSpec(memory_space=pltpu.VMEM)
    shape = jax.ShapeDtypeStruct
    square = (BLOCK, BLOCK)
    return pl.pallas_call(
        kernel,
        name="adjoint",
        out_shape=(
            shape((BLOCK, 128), F32), shape((64, BLOCK), F32), shape((2, 64, BLOCK), F32),
        ),
        in_specs=[anywhere] * 8,
        out_specs=[vmem] * 3,
        scratch_shapes=[
            pltpu.VMEM((BLOCK, 2048), BF16),
            pltpu.VMEM((2048, 1024), BF16),
            pltpu.VMEM((BLOCK, 1024), BF16),
            pltpu.VMEM(square, BF16),
            pltpu.VMEM((2, *square), BF16),
            pltpu.VMEM((2, *square), F32),
            pltpu.VMEM(square, BF16),
            pltpu.VMEM((2, *square), BF16),
            pltpu.VMEM((2048, BLOCK), BF16),
            pltpu.VMEM((2048, 1024), BF16),
            pltpu.VMEM((BLOCK, 1024), BF16),
            pltpu.VMEM((BLOCK, 1024), F32),
            pltpu.VMEM((BLOCK, 1024), F32),
            pltpu.VMEM((BLOCK, 1024), F32),
            pltpu.VMEM((6144, 128), F32),
            pltpu.VMEM((6144, 128), F32),
            pltpu.VMEM((3, 768, 128), F32),
            pltpu.VMEM((3, 192, 128), F32),
            pltpu.VMEM((7, 24, 128), F32),
            pltpu.VMEM((1024, 1024), BF16),
            pltpu.VMEM((1024, 1024), BF16),
            pltpu.VMEM((6, *square), BF16),
            pltpu.VMEM((3, *square), F32),
            pltpu.VMEM((2, 4, BLOCK, 128), F32),
            pltpu.VMEM((4, BLOCK, 128), F32),
            pltpu.VMEM((3, BLOCK, 128), F32),
            pltpu.VMEM((8, BLOCK, 128), F32),
            pltpu.VMEM((BLOCK, 128), F32),
            dma((10,)), dma((2, HOPS)), dma((HOPS,)), dma((2, HOPS)), dma((HOPS,)), dma((3,)), dma((3,)),
            dma((4,)), dma((4,)), dma((3,)), dma((3,)), dma((3,)), dma((3,)), dma((7,)), dma((7,)),
            dma((7,)), dma((7,)), dma((3,)), dma((3,)), dma((3,)), dma((3,)), dma((4,)), dma((4,)),
            dma((CHUNKS,)), dma((CHUNKS,)), dma, dma, dma((3,)), dma((3,)), dma((7, 4)), dma((4,)),
        ],
        compiler_params=pltpu.CompilerParams(
            collective_id=0, has_side_effects=True, vmem_limit_bytes=VMEM_BYTES
        ),
    )(trail, fac, xf, lf, li, grad, cg, dg)


def solution(mesh):
    fine = Mesh(mesh.devices.reshape(8, 4, 4, 2), ("z", "x", "y", "k"))
    row, col = ("z", "x"), ("y", "k")
    return jax.shard_map(
        shards,
        mesh=fine,
        in_specs=(P(row, col), P(col, None), P(), P(), P(), P(row, None), P(), P()),
        out_specs=(P(row, col), P(col, None), P(None, col, None)),
        check_vma=False,
    )
```

```python
import jax
import jax.numpy as jnp
from jax import lax
from jax.experimental import pallas as pl
from jax.experimental.pallas import tpu as pltpu
from jax.sharding import Mesh
from jax.sharding import PartitionSpec as P

MESH = pl.DeviceIdType.MESH
F32, BF16 = jnp.float32, jnp.bfloat16
BLOCK = 512
VMEM_BYTES = 62 * 1024 * 1024


def place():
    return tuple(lax.axis_index(a) for a in ("z", "x", "y", "k"))


def meet(peers):
    barrier = pltpu.get_barrier_semaphore()
    for peer in peers:
        pl.semaphore_signal(barrier, inc=1, device_id=peer, device_id_type=MESH)
    pl.semaphore_wait(barrier, len(peers))


def push(src, dst, send, recv, peer):
    return pltpu.make_async_remote_copy(
        src_ref=src, dst_ref=dst, send_sem=send, recv_sem=recv, device_id=peer, device_id_type=MESH
    )


def dot(a, b, ca=1, cb=0):
    return lax.dot_general(a, b, (((ca,), (cb,)), ((), ())), preferred_element_type=F32)


def split(a):
    high = a.astype(BF16)
    return high, (a - high.astype(F32)).astype(BF16)


def dot3(a, b, ca=1, cb=0):
    ah, al = a if isinstance(a, tuple) else split(a)
    bh, bl = b if isinstance(b, tuple) else split(b)
    return dot(ah, bh, ca, cb) + (dot(al, bh, ca, cb) + dot(ah, bl, ca, cb))


def dot2(a, b, ca=1, cb=0):
    if isinstance(a, tuple):
        return dot(a[0], b, ca, cb) + dot(a[1], b, ca, cb)
    return dot(a, b[0], ca, cb) + dot(a, b[1], ca, cb)


def symmetric(f):
    size = f.shape[0]
    rows = lax.broadcasted_iota(jnp.int32, (size, size), 0)
    cols = lax.broadcasted_iota(jnp.int32, (size, size), 1)
    halved = jnp.where(cols < rows, f, jnp.where(cols == rows, f * 0.5, 0.0))
    return halved + halved.T


def masked(m, row0, col0):
    rows = row0 + lax.broadcasted_iota(jnp.int32, m.shape, 0)
    cols = col0 + lax.broadcasted_iota(jnp.int32, m.shape, 1)
    scale = jnp.where(cols < rows, 1.0, jnp.where(cols == rows, 0.5, 0.0))
    return (m.astype(F32) * scale).astype(BF16)

CHUNKS = 32
SKEW = 4
LINES = BLOCK // CHUNKS
HOPS = 16


def kernel(
    trail, fac, xf, lf, li, grad, cg, dg,
    panel_out, cross_out, diag_out,
    m, fv, gv, xv, lfv, liv, cgv, dgv,
    mx, fz, f, mf, t, arrived, w, full, r1, r2, r3,
    ph, plo, pairs, consts, yp, q0, q1, tq, rt,
    ls, fs, fr, hs, hr, xs, xr,
    s0, v0, s1, v1, s2, v2, s3, v3, g3, u3, g2, u2, g1, u1, g0, u0,
    ts, tr, a0, b0, a1, b1s, es, er,
):
    z, x, y, k = place()
    c = 2 * y + k
    ys, ks = z >> 1, z & 1
    sibling = (z, x, y, 1 - k)
    lower = c <= z
    last = c == z
    chip_lower = 2 * y <= z
    source_chip = y == ys
    yn = (lax.rem(y + 3, 4), lax.rem(y + 1, 4))
    px = [lax.rem(x + d, 4) for d in (1, 2, 3)]
    py = [lax.rem(y + d, 4) for d in (1, 2, 3)]
    pz = [lax.rem(z + d, 8) for d in range(1, 8)]
    pc = [lax.rem(c + d, 8) for d in range(1, 8)]
    mine = pl.ds(pl.multiple_of(x * BLOCK, BLOCK), BLOCK)

    def local(n, src, dst):
        return pltpu.make_async_copy(src, dst, ls.at[n])

    get_trail = local(0, trail, m)
    get_factor = local(1, fac, fv)
    get_grad = local(2, grad, gv)
    get_small = [
        local(3, xf, xv), local(4, lf, lfv), local(5, li, liv), local(6, cg, cgv), local(7, dg, dgv)
    ]
    get_own = local(8, trail.at[:, mine], mx.at[mine, :])
    get_source = local(9, fac, fz)

    @pl.when(lower)
    def _():
        get_trail.start()
        get_factor.start()
        get_own.start()

    get_grad.start()
    for copy in get_small:
        copy.start()

    @pl.when(last)
    def _():
        get_source.start()

    meet(
        [(z, p, y, k) for p in px]
        + [(z, x, p >> 1, p & 1) for p in pc]
        + [(p, x, y, k) for p in pz]
    )

    def rows(s, i):
        block = lax.rem(x + i // 4, 4)
        return pl.ds(pl.multiple_of(block * BLOCK + s * 256 + lax.rem(i, 4) * 64, 64), 64)

    def first_hop(s, i):
        return push(
            fac.at[rows(s, i), :], fz.at[rows(s, i), :], fs.at[s, i], fr.at[i], (z, x, yn[s], s)
        )

    def beside_own(i):
        return push(fac.at[rows(1 - k, i), :], fz.at[rows(1 - k, i), :], hs.at[0, i], fr.at[i], sibling)

    def beside_other(i):
        return push(fac.at[rows(k, i), :], fz.at[rows(k, i), :], hs.at[1, i], hr.at[i], sibling)

    onward_y = jnp.where(k == 0, yn[0], yn[1])
    hops = jnp.where(k == 0, (ys - y + 4) & 3, (y - ys + 4) & 3)

    def forward(i):
        return push(
            fz.at[rows(k, i), :], fz.at[rows(k, i), :], fs.at[0, i], fr.at[i], (z, x, onward_y, k)
        )

    def share(i):
        return push(fz.at[rows(k, i), :], fz.at[rows(k, i), :], hs.at[0, i], hr.at[i], sibling)

    def other(i):
        return push(fz.at[rows(1 - k, i), :], fz.at[rows(1 - k, i), :], hs.at[0, i], hr.at[i], sibling)

    def across(d):
        return push(
            trail.at[:, pl.ds(pl.multiple_of(px[d] * BLOCK, 128), BLOCK)],
            mx.at[mine, :],
            xs.at[d],
            xr.at[d],
            (z, px[d], y, k),
        )

    def feed(lo, hi):
        if lo >= HOPS:
            return

        @pl.when(last)
        def _():
            @pl.loop(lo, min(hi, HOPS))
            def _(i):
                @pl.when(i >= 2)
                def _():
                    first_hop(0, i - 2).wait_send()
                    first_hop(1, i - 2).wait_send()

                first_hop(0, i).start()
                first_hop(1, i).start()
                beside_own(i).start()
                beside_other(i).start()

    feed(0, 2)

    @pl.when(lower)
    def _():
        for d in (2, 1, 0):
            across(d).start()

    def relays(lo, hi):
        feed(lo + 2, hi + 2)

        @pl.when(jnp.logical_not(source_chip))
        def _():
            @pl.loop(lo, hi)
            def _(i):
                forward(i).wait_recv()

                @pl.when(hops < 3)
                def _():
                    forward(i).start()

                share(i).start()

        @pl.when(source_chip & (k != ks))
        def _():
            @pl.loop(lo, hi)
            def _(i):
                forward(i).wait_recv()

    def others(lo, hi):
        @pl.when(jnp.logical_not(last))
        def _():
            @pl.loop(lo, hi)
            def _(i):
                other(i).wait_recv()

    @pl.when(lower)
    def _():
        get_trail.wait()
        get_factor.wait()

    def product(i):
        @pl.when(lower)
        def _():
            here = slice(i * 128, (i + 1) * 128)

            @pl.when(last)
            def _():
                m[here, :] = masked(m[here, :], x * BLOCK + i * 128, 0)

            mf[here, :] = dot(m[here, :], fv[...])

    @pl.when(c > z)
    def _():
        mf[...] = jnp.zeros_like(mf)
        w[...] = jnp.zeros_like(w)
        t[...] = jnp.zeros_like(t)

    for i in range(4):
        relays(i, i + 1)
        product(i)

    get_grad.wait()

    @pl.when(last)
    def _():
        get_source.wait()

    own = jnp.where(last, 1.0, 0.0)

    def add_block(block, a, b):
        @pl.when(lower)
        def _():
            mfa = mf[:, a * BLOCK : (a + 1) * BLOCK]
            mfb = mf[:, b * BLOCK : (b + 1) * BLOCK]
            ga = gv[:, a * BLOCK : (a + 1) * BLOCK].astype(F32) * own
            fa = f[:, a * BLOCK : (a + 1) * BLOCK]
            fb = f[:, b * BLOCK : (b + 1) * BLOCK]
            value = dot2(split(ga - mfa), fb, 0, 0) - dot2(fa, split(mfb), 0, 0)
            for j in range(4):
                w[pl.ds(j * 1536 + block * BLOCK, BLOCK), :] = value[:, j * 128 : (j + 1) * 128]

    half = k * 3072
    first = jnp.where(k == 0, y, x)
    second = jnp.where(k == 0, x, y)
    p1 = [lax.rem(first + d, 4) for d in (1, 2, 3)]
    p2 = [lax.rem(second + d, 4) for d in (1, 2, 3)]
    at1 = half + first * 768
    at2 = at1 + second * 192
    at3 = at2 + z * 24

    def part(at, n):
        return pl.ds(pl.multiple_of(at, 8), n)

    def along_first(p):
        return (z, jnp.where(k == 0, x, p), jnp.where(k == 0, p, y), k)

    def along_second(p):
        return (z, jnp.where(k == 0, p, x), jnp.where(k == 0, y, p), k)

    def out1(d):
        return push(w.at[part(half + p1[d] * 768, 768), :], r1.at[d], s1.at[d], v1.at[d], along_first(p1[d]))

    def out2(d):
        return push(w.at[part(at1 + p2[d] * 192, 192), :], r2.at[d], s2.at[d], v2.at[d], along_second(p2[d]))

    def out3(d):
        return push(w.at[part(at2 + pz[d] * 24, 24), :], r3.at[d], s3.at[d], v3.at[d], (pz[d], x, y, k))

    def whole(at, n, send, recv, peer):
        return push(full.at[part(at, n), :], full.at[part(at, n), :], send, recv, peer)

    def start(copies):
        for copy in copies:
            copy.start()

    def finish(copies):
        for copy in copies:
            copy.wait()

    def quarter(at, j):
        return part(at + lax.rem(j, 4) * 768, 768)

    def swapped(j):
        away = quarter(3072 - half, second + 1 + j)
        return push(w.at[away, :], full.at[away, :], s0.at[j], v0.at[j], sibling)

    c0 = [swapped(j) for j in range(4)]
    c1 = [out1(d) for d in range(3)]
    c2 = [out2(d) for d in range(3)]
    c3 = [out3(d) for d in range(7)]
    c4 = [whole(at3, 24, g3.at[d], u3.at[d], (pz[d], x, y, k)) for d in range(7)]
    c5 = [whole(at2, 192, g2.at[d], u2.at[d], along_second(p2[d])) for d in range(3)]
    c6 = [whole(at1, 768, g1.at[d], u1.at[d], along_first(p1[d])) for d in range(3)]
    c7 = [
        whole(half + lax.rem(first + 4 - j, 4) * 768, 768, g0.at[j], u0.at[j], sibling) for j in range(4)
    ]
    def pre_one():
        finish(get_small)
        ph[0:BLOCK, 0:BLOCK], plo[0:BLOCK, 0:BLOCK] = split(liv[0])
        ph[BLOCK:, BLOCK:], plo[BLOCK:, BLOCK:] = split(liv[1])
        ph[0:BLOCK, BLOCK:] = jnp.zeros((BLOCK, BLOCK), BF16)
        plo[0:BLOCK, BLOCK:] = jnp.zeros((BLOCK, BLOCK), BF16)

    def li0():
        return ph[0:BLOCK, 0:BLOCK], plo[0:BLOCK, 0:BLOCK]

    def li1():
        return ph[BLOCK:, BLOCK:], plo[BLOCK:, BLOCK:]

    def minus_b1():
        return ph[BLOCK:, 0:BLOCK], plo[BLOCK:, 0:BLOCK]

    def pair(n):
        return pairs[2 * n], pairs[2 * n + 1]

    def keep(n, value):
        pairs[2 * n], pairs[2 * n + 1] = split(value)

    def pre_cross():
        keep(0, dot2(li1(), xv[...]))

    def pre_b1():
        high, low = split(dot3(pair(0), li0()))
        ph[BLOCK:, 0:BLOCK], plo[BLOCK:, 0:BLOCK] = -high, -low

    def pre_j0():
        keep(0, dot2(li0(), lfv[0]))

    def pre_j1():
        keep(1, dot2(li1(), lfv[1]))

    def pre_b2():
        keep(2, -dot2(minus_b1(), lfv[0]))

    def pre_three():
        consts[0] = dot(lfv[0], dgv[0], 0, 0)
        consts[1] = dot(lfv[1], dgv[1], 0, 0)
        consts[2] = dot2(cgv[...], pair(0))

    def transposed(j):
        @pl.when(lower)
        def _():
            if j == 0:
                get_own.wait()
            else:
                across(3 - j).wait_recv()
            block = lax.rem(x + j, 4)
            here = pl.ds(pl.multiple_of(block * BLOCK, BLOCK), BLOCK)

            @pl.when(last)
            def _():
                mx[here, :] = masked(mx[here, :], block * BLOCK, x * BLOCK)

            @pl.loop(0, 2)
            def _(i):
                lines = pl.ds(pl.multiple_of(i * 256, 256), 256)
                value = dot(mx[here, lines], fz[here, :], 0, 0)
                if j == 0:
                    t[lines, :] = value
                else:
                    t[lines, :] += value

    def ready():
        others(0, 4)

        @pl.when(lower)
        def _():
            f[...] = fz[mine, :]

    between = {
        4: [pre_one],
        5: [pre_cross],
        6: [pre_b1],
        7: [ready, lambda: add_block(0, 1, 1)],
        8: [lambda: add_block(1, 1, 0)],
        9: [lambda: add_block(2, 0, 0), lambda: start(c0)],
        10: [pre_j0],
        11: [pre_j1],
        12: [pre_b2],
        13: [lambda: others(4, 8)],
        14: [lambda: transposed(0)],
    }
    for i in range(4, HOPS):
        relays(i, i + 1)
        for piece in between.get(i, []):
            piece()
    for j in range(4):
        c0[j].wait_recv()
        here = quarter(half, first + 1 + j)
        w[here, :] += full[here, :]
        if j < 3:
            c1[j].start()
    transposed(1)
    others(8, 12)
    transposed(2)
    others(12, 16)
    transposed(3)

    before, after = lax.rem(z + 7, 8), lax.rem(z + 1, 8)
    position = jnp.where(k == 0, 7 - z, (z - c + 7) & 7)
    taking = (k == 1) | lower
    onward_z = jnp.where(k == 0, before, after)

    def chunk(i):
        here = pl.ds(pl.multiple_of(i * LINES, LINES), LINES)
        return push(t.at[here, :], arrived.at[here, :], ts.at[i], tr.at[i], (onward_z, x, y, k))

    def mapped(part_rows, store):
        h, l = split(part_rows)
        low = dot3((h, l), (ph[:, :BLOCK], plo[:, :BLOCK]))
        high = dot3((h[:, BLOCK:], l[:, BLOCK:]), (ph[BLOCK:, BLOCK:], plo[BLOCK:, BLOCK:]))
        for g in range(4):
            store(g, low[:, g * 128 : (g + 1) * 128])
            store(g + 4, high[:, g * 128 : (g + 1) * 128])

    def direct(i):
        @pl.when(chip_lower)
        def _():
            here = slice(i * 128, (i + 1) * 128)

            def store(g, value):
                yp[g % 2, g // 2, here, :] = value

            mapped(mf[here, :], store)

    swap = push(yp.at[1 - k], q0, a0, b0, sibling)

    def spread(d):
        return push(yp.at[k, py[d]], q1.at[d], a1.at[d], b1s.at[d], (z, x, py[d], k))

    def swap_start():
        @pl.when(chip_lower)
        def _():
            swap.start()

    def swap_end():
        @pl.when(chip_lower)
        def _():
            swap.wait()
            yp[pl.ds(k, 1)] += q0[...][None]
            for d in range(3):
                spread(d).start()

    def scatter(d, i):
        here = pl.ds(pl.multiple_of(i * 128, 128), 128)
        to = pc[d]
        return push(tq.at[to, here, :], rt.at[here, :], es.at[d, i], er.at[i], (z, x, to >> 1, to & 1))

    def last_part(i):
        here = pl.ds(pl.multiple_of(i * 128, 128), 128)

        def store(g, value):
            tq[g, here, :] = value

        mapped(t[here, :], store)
        for d in range(7):
            scatter(d, i).start()

    def chain(s):
        i = s - SKEW * position

        @pl.when(taking & (i >= 0) & (i < CHUNKS))
        def _():
            here = pl.ds(pl.multiple_of(i * LINES, LINES), LINES)

            @pl.when(position > 0)
            def _():
                chunk(i).wait_recv()
                t[here, :] += arrived[here, :]

            @pl.when(jnp.logical_not(last))
            def _():
                @pl.when(i >= 4)
                def _():
                    chunk(i - 4).wait_send()

                chunk(i).start()

            @pl.when(last & (lax.rem(i, 8) == 7))
            def _():
                last_part(i >> 3)

    def sum_one():
        finish(c1)
        w[part(at1, 768), :] += r1[0] + r1[1] + r1[2]
        start(c2)

    def sum_two():
        finish(c2)
        w[part(at2, 192), :] += r2[0] + r2[1] + r2[2]
        start(c3)

    def sum_three():
        finish(c3)
        full[part(at3, 24), :] = w[part(at3, 24), :] + (
            ((r3[0] + r3[1]) + (r3[2] + r3[3])) + ((r3[4] + r3[5]) + r3[6])
        )
        start(c4)

    def then(done, go):
        def run():
            finish(done)
            start(go)

        return run

    def gather_one():
        finish(c5)
        start(c6)
        c7[0].start()

    def gather_two():
        for d in range(3):
            c6[d].wait_recv()
            c7[d + 1].start()

    beside = {
        1: lambda: direct(0),
        4: lambda: direct(1),
        7: lambda: direct(2),
        10: lambda: direct(3),
        11: swap_start,
        13: sum_one,
        19: sum_two,
        22: swap_end,
        25: sum_three,
        28: pre_three,
        31: then(c4, c5),
        37: gather_one,
        51: gather_two,
    }

    @pl.loop(0, CHUNKS + 7 * SKEW)
    def _(s):
        chain(s)
        for at, step in beside.items():
            pl.when(s == at)(step)

    for copy in c0 + c6:
        copy.wait_send()
    finish(c7)

    def load(block):
        return split(
            jnp.concatenate([full[pl.ds(j * 1536 + block * BLOCK, BLOCK), :] for j in range(4)], axis=1)
        )

    w11, w10, w00 = load(0), load(1), load(2)
    slab = pl.ds(pl.multiple_of(c * 64, 64), 64)
    pick = jnp.where(
        lax.broadcasted_iota(jnp.int32, (BLOCK, 64), 0)
        == c * 64 + lax.broadcasted_iota(jnp.int32, (BLOCK, 64), 1),
        1.0,
        0.0,
    ).astype(BF16)

    def turned(parts):
        return tuple(dot(pick, part_of, 0, 1).astype(BF16) for part_of in parts)

    lit1, lit0 = turned(li1()), turned(li0())
    sym1 = split(symmetric(consts[1] - dot3(pair(1), w11, 0, 0)))
    inner = split(dot3(w10, pair(0)) + dot3(sym1, pair(2)))
    cl = split(consts[2] - dot3(li1(), inner, 0, 0))
    g_zero = consts[0] - dot3(pair(0), w00, 0, 0) + dot3(pair(2), w10, 0, 0) - dot2(cl, xv[...], 0, 0)
    sym0 = split(symmetric(g_zero))
    ls1 = split(dot3(lit1, sym1))
    diag_out[1] = dot3(ls1, li1())
    cross_out[...] = dot2(cgv[slab, :], li0()) - (
        dot3(split(dot3(lit1, w10)), li0()) - dot3(ls1, minus_b1())
    )
    diag_out[0] = dot3(split(dot3(lit0, sym0)), li0())

    cols = pl.ds(pl.multiple_of(c * 128, 128), 128)
    panel_out[...] = dot2(gv[...], (ph[:, cols], plo[:, cols]))

    @pl.when(chip_lower)
    def _():
        panel_out[...] -= yp[k, y]

    for d in range(3):
        @pl.when(2 * lax.rem(y + 3 - d, 4) <= z)
        def _():
            spread(d).wait_recv()
            panel_out[...] -= q1[d]

    @pl.when(last)
    def _():
        panel_out[...] -= tq[c]

    @pl.when(jnp.logical_not(last))
    def _():
        for i in range(4):
            scatter(0, i).wait_recv()
        panel_out[...] -= rt[...]

    @pl.when(last)
    def _():
        @pl.loop(0, HOPS)
        def _(i):
            beside_own(i).wait_send()
            beside_other(i).wait_send()

        for i in (HOPS - 2, HOPS - 1):
            first_hop(0, i).wait_send()
            first_hop(1, i).wait_send()

        for i in range(4):
            for d in range(7):
                scatter(d, i).wait_send()

    @pl.when(jnp.logical_not(source_chip))
    def _():
        @pl.loop(0, HOPS)
        def _(i):
            share(i).wait_send()

            @pl.when(hops < 3)
            def _():
                forward(i).wait_send()

    @pl.when(lower)
    def _():
        for d in range(3):
            across(d).wait_send()

    @pl.when(taking & jnp.logical_not(last))
    def _():
        for i in range(CHUNKS - 4, CHUNKS):
            chunk(i).wait_send()

    @pl.when(chip_lower)
    def _():
        for d in range(3):
            spread(d).wait_send()


def copy_kernel(a, b, c, out_a, out_b, out_c):
    out_a[...], out_b[...], out_c[...] = a[...], b[...], c[...]


def shards(trail, fac, xf, lf, li, grad, cg, dg):
    dma = pltpu.SemaphoreType.DMA
    anywhere = pl.BlockSpec(memory_space=pl.ANY)
    vmem = pl.BlockSpec(memory_space=pltpu.VMEM)
    shape = jax.ShapeDtypeStruct
    square = (BLOCK, BLOCK)
    results = (
        shape((BLOCK, 128), F32), shape((64, BLOCK), F32), shape((2, 64, BLOCK), F32),
    )
    made = pl.pallas_call(
        kernel,
        name="adjoint",
        out_shape=results,
        in_specs=[anywhere] * 8,
        out_specs=[vmem] * 3,
        scratch_shapes=[
            pltpu.VMEM((BLOCK, 2048), BF16),
            pltpu.VMEM((2048, 1024), BF16),
            pltpu.VMEM((BLOCK, 1024), BF16),
            pltpu.VMEM(square, BF16),
            pltpu.VMEM((2, *square), BF16),
            pltpu.VMEM((2, *square), F32),
            pltpu.VMEM(square, BF16),
            pltpu.VMEM((2, *square), BF16),
            pltpu.VMEM((2048, BLOCK), BF16),
            pltpu.VMEM((2048, 1024), BF16),
            pltpu.VMEM((BLOCK, 1024), BF16),
            pltpu.VMEM((BLOCK, 1024), F32),
            pltpu.VMEM((BLOCK, 1024), F32),
            pltpu.VMEM((BLOCK, 1024), F32),
            pltpu.VMEM((6144, 128), F32),
            pltpu.VMEM((6144, 128), F32),
            pltpu.VMEM((3, 768, 128), F32),
            pltpu.VMEM((3, 192, 128), F32),
            pltpu.VMEM((7, 24, 128), F32),
            pltpu.VMEM((1024, 1024), BF16),
            pltpu.VMEM((1024, 1024), BF16),
            pltpu.VMEM((6, *square), BF16),
            pltpu.VMEM((3, *square), F32),
            pltpu.VMEM((2, 4, BLOCK, 128), F32),
            pltpu.VMEM((4, BLOCK, 128), F32),
            pltpu.VMEM((3, BLOCK, 128), F32),
            pltpu.VMEM((8, BLOCK, 128), F32),
            pltpu.VMEM((BLOCK, 128), F32),
            dma((10,)), dma((2, HOPS)), dma((HOPS,)), dma((2, HOPS)), dma((HOPS,)), dma((3,)), dma((3,)),
            dma((4,)), dma((4,)), dma((3,)), dma((3,)), dma((3,)), dma((3,)), dma((7,)), dma((7,)),
            dma((7,)), dma((7,)), dma((3,)), dma((3,)), dma((3,)), dma((3,)), dma((4,)), dma((4,)),
            dma((CHUNKS,)), dma((CHUNKS,)), dma, dma, dma((3,)), dma((3,)), dma((7, 4)), dma((4,)),
        ],
        compiler_params=pltpu.CompilerParams(
            collective_id=0, has_side_effects=True, vmem_limit_bytes=VMEM_BYTES
        ),
    )(trail, fac, xf, lf, li, grad, cg, dg)
    return pl.pallas_call(
        copy_kernel, name="results", out_shape=results, in_specs=[vmem] * 3, out_specs=[vmem] * 3
    )(*made)


def solution(mesh):
    fine = Mesh(mesh.devices.reshape(8, 4, 4, 2), ("z", "x", "y", "k"))
    row, col = ("z", "x"), ("y", "k")
    return jax.shard_map(
        shards,
        mesh=fine,
        in_specs=(P(row, col), P(col, None), P(), P(), P(), P(row, None), P(), P()),
        out_specs=(P(row, col), P(col, None), P(None, col, None)),
        check_vma=False,
    )
```

```python
import jax
import jax.numpy as jnp
from jax import lax
from jax.experimental import pallas as pl
from jax.experimental.pallas import tpu as pltpu
from jax.sharding import Mesh
from jax.sharding import PartitionSpec as P

MESH = pl.DeviceIdType.MESH
F32, BF16 = jnp.float32, jnp.bfloat16
BLOCK = 512
VMEM_BYTES = 62 * 1024 * 1024


def place():
    return tuple(lax.axis_index(a) for a in ("z", "x", "y", "k"))


def meet(peers):
    barrier = pltpu.get_barrier_semaphore()
    for peer in peers:
        pl.semaphore_signal(barrier, inc=1, device_id=peer, device_id_type=MESH)
    pl.semaphore_wait(barrier, len(peers))


def push(src, dst, send, recv, peer):
    return pltpu.make_async_remote_copy(
        src_ref=src, dst_ref=dst, send_sem=send, recv_sem=recv, device_id=peer, device_id_type=MESH
    )


def dot(a, b, ca=1, cb=0):
    return lax.dot_general(a, b, (((ca,), (cb,)), ((), ())), preferred_element_type=F32)


def split(a):
    high = a.astype(BF16)
    return high, (a - high.astype(F32)).astype(BF16)


def dot3(a, b, ca=1, cb=0):
    ah, al = a if isinstance(a, tuple) else split(a)
    bh, bl = b if isinstance(b, tuple) else split(b)
    return dot(ah, bh, ca, cb) + (dot(al, bh, ca, cb) + dot(ah, bl, ca, cb))


def dot2(a, b, ca=1, cb=0):
    if isinstance(a, tuple):
        return dot(a[0], b, ca, cb) + dot(a[1], b, ca, cb)
    return dot(a, b[0], ca, cb) + dot(a, b[1], ca, cb)


def symmetric(f):
    size = f.shape[0]
    rows = lax.broadcasted_iota(jnp.int32, (size, size), 0)
    cols = lax.broadcasted_iota(jnp.int32, (size, size), 1)
    halved = jnp.where(cols < rows, f, jnp.where(cols == rows, f * 0.5, 0.0))
    return halved + halved.T


def masked(m, row0, col0):
    rows = row0 + lax.broadcasted_iota(jnp.int32, m.shape, 0)
    cols = col0 + lax.broadcasted_iota(jnp.int32, m.shape, 1)
    scale = jnp.where(cols < rows, 1.0, jnp.where(cols == rows, 0.5, 0.0))
    return (m.astype(F32) * scale).astype(BF16)

CHUNKS = 32
SKEW = 4
LINES = BLOCK // CHUNKS
HOPS = 16


def kernel(
    trail, fac, xf, lf, li, grad, cg, dg,
    panel_out, cross_out, diag_out,
    m, fv, gv, xv, lfv, liv, cgv, dgv,
    mx, fz, f, mf, t, arrived, w, full, r1, r2, r3,
    ph, plo, pairs, consts, yp, q0, q1, tq, rt,
    ls, fs, fr, hs, hr, xs, xr,
    s0, v0, s1, v1, s2, v2, s3, v3, g3, u3, g2, u2, g1, u1, g0, u0,
    ts, tr, a0, b0, a1, b1s, es, er,
):
    z, x, y, k = place()
    c = 2 * y + k
    ys, ks = z >> 1, z & 1
    sibling = (z, x, y, 1 - k)
    lower = c <= z
    last = c == z
    chip_lower = 2 * y <= z
    source_chip = y == ys
    yn = (lax.rem(y + 3, 4), lax.rem(y + 1, 4))
    px = [lax.rem(x + d, 4) for d in (1, 2, 3)]
    py = [lax.rem(y + d, 4) for d in (1, 2, 3)]
    pz = [lax.rem(z + d, 8) for d in range(1, 8)]
    pc = [lax.rem(c + d, 8) for d in range(1, 8)]
    mine = pl.ds(pl.multiple_of(x * BLOCK, BLOCK), BLOCK)

    def local(n, src, dst):
        return pltpu.make_async_copy(src, dst, ls.at[n])

    get_trail = local(0, trail, m)
    get_factor = local(1, fac, fv)
    get_grad = local(2, grad, gv)
    get_small = [
        local(3, xf, xv), local(4, lf, lfv), local(5, li, liv), local(6, cg, cgv), local(7, dg, dgv)
    ]
    get_own = local(8, trail.at[:, mine], mx.at[mine, :])
    get_source = local(9, fac, fz)

    @pl.when(lower)
    def _():
        get_trail.start()
        get_factor.start()
        get_own.start()

    get_grad.start()
    for copy in get_small:
        copy.start()

    @pl.when(last)
    def _():
        get_source.start()

    meet(
        [(z, p, y, k) for p in px]
        + [(z, x, p >> 1, p & 1) for p in pc]
        + [(p, x, y, k) for p in pz]
    )

    def rows(s, i):
        block = lax.rem(x + i // 4, 4)
        return pl.ds(pl.multiple_of(block * BLOCK + s * 256 + lax.rem(i, 4) * 64, 64), 64)

    def first_hop(s, i):
        return push(
            fac.at[rows(s, i), :], fz.at[rows(s, i), :], fs.at[s, i], fr.at[i], (z, x, yn[s], s)
        )

    def beside_own(i):
        return push(fac.at[rows(1 - k, i), :], fz.at[rows(1 - k, i), :], hs.at[0, i], fr.at[i], sibling)

    def beside_other(i):
        return push(fac.at[rows(k, i), :], fz.at[rows(k, i), :], hs.at[1, i], hr.at[i], sibling)

    onward_y = jnp.where(k == 0, yn[0], yn[1])
    hops = jnp.where(k == 0, (ys - y + 4) & 3, (y - ys + 4) & 3)

    def forward(i):
        return push(
            fz.at[rows(k, i), :], fz.at[rows(k, i), :], fs.at[0, i], fr.at[i], (z, x, onward_y, k)
        )

    def share(i):
        return push(fz.at[rows(k, i), :], fz.at[rows(k, i), :], hs.at[0, i], hr.at[i], sibling)

    def other(i):
        return push(fz.at[rows(1 - k, i), :], fz.at[rows(1 - k, i), :], hs.at[0, i], hr.at[i], sibling)

    def across(d):
        return push(
            trail.at[:, pl.ds(pl.multiple_of(px[d] * BLOCK, 128), BLOCK)],
            mx.at[mine, :],
            xs.at[d],
            xr.at[d],
            (z, px[d], y, k),
        )

    def feed(lo, hi):
        if lo >= HOPS:
            return

        @pl.when(last)
        def _():
            @pl.loop(lo, min(hi, HOPS))
            def _(i):
                @pl.when(i >= 2)
                def _():
                    first_hop(0, i - 2).wait_send()
                    first_hop(1, i - 2).wait_send()

                first_hop(0, i).start()
                first_hop(1, i).start()
                beside_own(i).start()
                beside_other(i).start()

    feed(0, 2)

    @pl.when(lower)
    def _():
        for d in (2, 1, 0):
            across(d).start()

    def relays(lo, hi):
        feed(lo + 2, hi + 2)

        @pl.when(jnp.logical_not(source_chip))
        def _():
            @pl.loop(lo, hi)
            def _(i):
                forward(i).wait_recv()

                @pl.when(hops < 3)
                def _():
                    forward(i).start()

                share(i).start()

        @pl.when(source_chip & (k != ks))
        def _():
            @pl.loop(lo, hi)
            def _(i):
                forward(i).wait_recv()

    def others(lo, hi):
        @pl.when(jnp.logical_not(last))
        def _():
            @pl.loop(lo, hi)
            def _(i):
                other(i).wait_recv()

    @pl.when(lower)
    def _():
        get_trail.wait()
        get_factor.wait()

    def product(i):
        @pl.when(lower)
        def _():
            here = slice(i * 128, (i + 1) * 128)

            @pl.when(last)
            def _():
                m[here, :] = masked(m[here, :], x * BLOCK + i * 128, 0)

            mf[here, :] = dot(m[here, :], fv[...])

    @pl.when(c > z)
    def _():
        mf[...] = jnp.zeros_like(mf)
        w[...] = jnp.zeros_like(w)
        t[...] = jnp.zeros_like(t)

    for i in range(4):
        relays(i, i + 1)
        product(i)

    get_grad.wait()

    @pl.when(last)
    def _():
        get_source.wait()

    own = jnp.where(last, 1.0, 0.0)

    def add_block(block, a, b):
        @pl.when(lower)
        def _():
            mfa = mf[:, a * BLOCK : (a + 1) * BLOCK]
            mfb = mf[:, b * BLOCK : (b + 1) * BLOCK]
            ga = gv[:, a * BLOCK : (a + 1) * BLOCK].astype(F32) * own
            fa = f[:, a * BLOCK : (a + 1) * BLOCK]
            fb = f[:, b * BLOCK : (b + 1) * BLOCK]
            value = dot2(split(ga - mfa), fb, 0, 0) - dot2(fa, split(mfb), 0, 0)
            for j in range(4):
                w[pl.ds(j * 1536 + block * BLOCK, BLOCK), :] = value[:, j * 128 : (j + 1) * 128]

    half = k * 3072
    first = jnp.where(k == 0, y, x)
    second = jnp.where(k == 0, x, y)
    p1 = [lax.rem(first + d, 4) for d in (1, 2, 3)]
    p2 = [lax.rem(second + d, 4) for d in (1, 2, 3)]
    at1 = half + first * 768
    at2 = at1 + second * 192
    at3 = at2 + z * 24

    def part(at, n):
        return pl.ds(pl.multiple_of(at, 8), n)

    def along_first(p):
        return (z, jnp.where(k == 0, x, p), jnp.where(k == 0, p, y), k)

    def along_second(p):
        return (z, jnp.where(k == 0, p, x), jnp.where(k == 0, y, p), k)

    def out1(d):
        return push(w.at[part(half + p1[d] * 768, 768), :], r1.at[d], s1.at[d], v1.at[d], along_first(p1[d]))

    def out2(d):
        return push(w.at[part(at1 + p2[d] * 192, 192), :], r2.at[d], s2.at[d], v2.at[d], along_second(p2[d]))

    def out3(d):
        return push(w.at[part(at2 + pz[d] * 24, 24), :], r3.at[d], s3.at[d], v3.at[d], (pz[d], x, y, k))

    def whole(at, n, send, recv, peer):
        return push(full.at[part(at, n), :], full.at[part(at, n), :], send, recv, peer)

    def start(copies):
        for copy in copies:
            copy.start()

    def finish(copies):
        for copy in copies:
            copy.wait()

    def quarter(at, j):
        return part(at + lax.rem(j, 4) * 768, 768)

    def swapped(j):
        away = quarter(3072 - half, second + 1 + j)
        return push(w.at[away, :], full.at[away, :], s0.at[j], v0.at[j], sibling)

    c0 = [swapped(j) for j in range(4)]
    c1 = [out1(d) for d in range(3)]
    c2 = [out2(d) for d in range(3)]
    c3 = [out3(d) for d in range(7)]
    c4 = [whole(at3, 24, g3.at[d], u3.at[d], (pz[d], x, y, k)) for d in range(7)]
    c5 = [whole(at2, 192, g2.at[d], u2.at[d], along_second(p2[d])) for d in range(3)]
    c6 = [whole(at1, 768, g1.at[d], u1.at[d], along_first(p1[d])) for d in range(3)]
    c7 = [
        whole(half + lax.rem(first + 4 - j, 4) * 768, 768, g0.at[j], u0.at[j], sibling) for j in range(4)
    ]
    def sum_one():
        finish(c1)
        w[part(at1, 768), :] += r1[0] + r1[1] + r1[2]
        start(c2)

    def pre_one():
        finish(get_small)
        ph[0:BLOCK, 0:BLOCK], plo[0:BLOCK, 0:BLOCK] = split(liv[0])
        ph[BLOCK:, BLOCK:], plo[BLOCK:, BLOCK:] = split(liv[1])
        ph[0:BLOCK, BLOCK:] = jnp.zeros((BLOCK, BLOCK), BF16)
        plo[0:BLOCK, BLOCK:] = jnp.zeros((BLOCK, BLOCK), BF16)

    def li0():
        return ph[0:BLOCK, 0:BLOCK], plo[0:BLOCK, 0:BLOCK]

    def li1():
        return ph[BLOCK:, BLOCK:], plo[BLOCK:, BLOCK:]

    def minus_b1():
        return ph[BLOCK:, 0:BLOCK], plo[BLOCK:, 0:BLOCK]

    def pair(n):
        return pairs[2 * n], pairs[2 * n + 1]

    def keep(n, value):
        pairs[2 * n], pairs[2 * n + 1] = split(value)

    def pre_cross():
        keep(0, dot2(li1(), xv[...]))

    def pre_b1():
        high, low = split(dot3(pair(0), li0()))
        ph[BLOCK:, 0:BLOCK], plo[BLOCK:, 0:BLOCK] = -high, -low

    def pre_j0():
        keep(0, dot2(li0(), lfv[0]))

    def pre_j1():
        keep(1, dot2(li1(), lfv[1]))

    def pre_b2():
        keep(2, -dot2(minus_b1(), lfv[0]))

    def pre_three():
        consts[0] = dot(lfv[0], dgv[0], 0, 0)
        consts[1] = dot(lfv[1], dgv[1], 0, 0)
        consts[2] = dot2(cgv[...], pair(0))

    def transposed(j):
        @pl.when(lower)
        def _():
            if j == 0:
                get_own.wait()
            else:
                across(3 - j).wait_recv()
            block = lax.rem(x + j, 4)
            here = pl.ds(pl.multiple_of(block * BLOCK, BLOCK), BLOCK)

            @pl.when(last)
            def _():
                mx[here, :] = masked(mx[here, :], block * BLOCK, x * BLOCK)

            @pl.loop(0, 2)
            def _(i):
                lines = pl.ds(pl.multiple_of(i * 256, 256), 256)
                value = dot(mx[here, lines], fz[here, :], 0, 0)
                if j == 0:
                    t[lines, :] = value
                else:
                    t[lines, :] += value

    def ready():
        others(0, 4)

        @pl.when(lower)
        def _():
            f[...] = fz[mine, :]

    def pass_on(j):
        c0[j].wait_recv()
        here = quarter(half, first + 1 + j)
        w[here, :] += full[here, :]
        if j < 3:
            c1[j].start()

    between = {
        7: [ready, lambda: add_block(0, 1, 1)],
        8: [lambda: add_block(1, 1, 0)],
        9: [lambda: add_block(2, 0, 0), lambda: start(c0)],
        10: [pre_one],
        11: [lambda: pass_on(0), lambda: pass_on(1)],
        12: [lambda: pass_on(2), lambda: pass_on(3), pre_cross],
        13: [lambda: others(4, 8), pre_b1],
        14: [lambda: transposed(0)],
    }
    for i in range(4, HOPS):
        relays(i, i + 1)
        for piece in between.get(i, []):
            piece()
    transposed(1)
    others(8, 12)
    sum_one()
    transposed(2)
    others(12, 16)
    transposed(3)

    before, after = lax.rem(z + 7, 8), lax.rem(z + 1, 8)
    position = jnp.where(k == 0, 7 - z, (z - c + 7) & 7)
    taking = (k == 1) | lower
    onward_z = jnp.where(k == 0, before, after)

    def chunk(i):
        here = pl.ds(pl.multiple_of(i * LINES, LINES), LINES)
        return push(t.at[here, :], arrived.at[here, :], ts.at[i], tr.at[i], (onward_z, x, y, k))

    def mapped(part_rows, store):
        h, l = split(part_rows)
        low = dot3((h, l), (ph[:, :BLOCK], plo[:, :BLOCK]))
        high = dot3((h[:, BLOCK:], l[:, BLOCK:]), (ph[BLOCK:, BLOCK:], plo[BLOCK:, BLOCK:]))
        for g in range(4):
            store(g, low[:, g * 128 : (g + 1) * 128])
            store(g + 4, high[:, g * 128 : (g + 1) * 128])

    def direct(i):
        @pl.when(chip_lower)
        def _():
            here = slice(i * 128, (i + 1) * 128)

            def store(g, value):
                yp[g % 2, g // 2, here, :] = value

            mapped(mf[here, :], store)

    swap = push(yp.at[1 - k], q0, a0, b0, sibling)

    def spread(d):
        return push(yp.at[k, py[d]], q1.at[d], a1.at[d], b1s.at[d], (z, x, py[d], k))

    def swap_start():
        @pl.when(chip_lower)
        def _():
            swap.start()

    def swap_end():
        @pl.when(chip_lower)
        def _():
            swap.wait()
            yp[pl.ds(k, 1)] += q0[...][None]
            for d in range(3):
                spread(d).start()

    def scatter(d, i):
        here = pl.ds(pl.multiple_of(i * 128, 128), 128)
        to = pc[d]
        return push(tq.at[to, here, :], rt.at[here, :], es.at[d, i], er.at[i], (z, x, to >> 1, to & 1))

    def last_part(i):
        here = pl.ds(pl.multiple_of(i * 128, 128), 128)

        def store(g, value):
            tq[g, here, :] = value

        mapped(t[here, :], store)
        for d in range(7):
            scatter(d, i).start()

    def chain(s):
        i = s - SKEW * position

        @pl.when(taking & (i >= 0) & (i < CHUNKS))
        def _():
            here = pl.ds(pl.multiple_of(i * LINES, LINES), LINES)

            @pl.when(position > 0)
            def _():
                chunk(i).wait_recv()
                t[here, :] += arrived[here, :]

            @pl.when(jnp.logical_not(last))
            def _():
                @pl.when(i >= 4)
                def _():
                    chunk(i - 4).wait_send()

                chunk(i).start()

            @pl.when(last & (lax.rem(i, 8) == 7))
            def _():
                last_part(i >> 3)

    def sum_two():
        finish(c2)
        w[part(at2, 192), :] += r2[0] + r2[1] + r2[2]
        start(c3)

    def sum_three():
        finish(c3)
        full[part(at3, 24), :] = w[part(at3, 24), :] + (
            ((r3[0] + r3[1]) + (r3[2] + r3[3])) + ((r3[4] + r3[5]) + r3[6])
        )
        start(c4)

    def then(done, go):
        def run():
            finish(done)
            start(go)

        return run

    def gather_one():
        finish(c5)
        start(c6)
        c7[0].start()

    def gather_two():
        for d in range(3):
            c6[d].wait_recv()
            c7[d + 1].start()

    def square(n):
        return pl.ds(n // 2 * BLOCK, BLOCK), pl.ds(n % 2 * BLOCK, BLOCK)

    def hold(n, value):
        fv[square(2 * n)], fv[square(2 * n + 1)] = split(value)

    def held(n):
        return fv[square(2 * n)], fv[square(2 * n + 1)]

    def total(block):
        return jnp.concatenate(
            [full[pl.ds(j * 1536 + block * BLOCK, BLOCK), :] for j in range(4)], axis=1
        )

    slab = pl.ds(pl.multiple_of(c * 64, 64), 64)

    def turned(parts):
        pick = jnp.where(
            lax.broadcasted_iota(jnp.int32, (BLOCK, 64), 0)
            == c * 64 + lax.broadcasted_iota(jnp.int32, (BLOCK, 64), 1),
            1.0,
            0.0,
        ).astype(BF16)
        return tuple(dot(pick, part_of, 0, 1).astype(BF16) for part_of in parts)

    def dense_one():
        hold(0, symmetric(consts[1] - dot3(pair(1), split(total(0)), 0, 0)))

    def dense_two():
        hold(1, total(1))
        mf[:, 0:BLOCK] = dot3(held(1), pair(0))

    def dense_three():
        hold(2, mf[:, 0:BLOCK] + dot3(held(0), pair(2)))

    def dense_four():
        hold(3, consts[2] - dot3(li1(), held(2), 0, 0))

    def dense_five():
        mf[:, BLOCK:] = consts[0] - dot3(pair(0), split(total(2)), 0, 0)

    def dense_six():
        mf[:, BLOCK:] += dot3(pair(2), held(1), 0, 0)

    def dense_seven():
        hold(2, symmetric(mf[:, BLOCK:] - dot2(held(3), xv[...], 0, 0)))

    def dense_eight():
        lit1 = turned(li1())
        ls1 = split(dot3(lit1, held(0)))
        diag_out[1] = dot3(ls1, li1())
        cross_out[...] = dot2(cgv[slab, :], li0()) - (
            dot3(split(dot3(lit1, held(1))), li0()) - dot3(ls1, minus_b1())
        )

    def dense_nine():
        diag_out[0] = dot3(split(dot3(turned(li0()), held(2))), li0())

    cols = pl.ds(pl.multiple_of(c * 128, 128), 128)

    def own_gradient():
        panel_out[...] = dot2(gv[...], (ph[:, cols], plo[:, cols]))

    beside = {
        0: sum_two,
        1: lambda: direct(0),
        3: lambda: direct(1),
        6: sum_three,
        7: lambda: direct(2),
        9: lambda: direct(3),
        10: swap_start,
        12: then(c4, c5),
        14: pre_j0,
        16: pre_j1,
        18: gather_one,
        20: pre_b2,
        22: swap_end,
        25: pre_three,
        28: own_gradient,
        33: gather_two,
        37: then(c7, []),
        38: dense_one,
        40: dense_two,
        42: dense_three,
        44: dense_four,
        46: dense_five,
        48: dense_six,
        50: dense_seven,
        52: dense_eight,
        54: dense_nine,
    }

    @pl.loop(0, CHUNKS + 7 * SKEW)
    def _(s):
        chain(s)
        for at, step in beside.items():
            pl.when(s == at)(step)

    for copy in c0 + c6:
        copy.wait_send()
    @pl.when(chip_lower)
    def _():
        panel_out[...] -= yp[k, y]

    for d in range(3):
        @pl.when(2 * lax.rem(y + 3 - d, 4) <= z)
        def _():
            spread(d).wait_recv()
            panel_out[...] -= q1[d]

    @pl.when(last)
    def _():
        panel_out[...] -= tq[c]

    @pl.when(jnp.logical_not(last))
    def _():
        for i in range(4):
            scatter(0, i).wait_recv()
        panel_out[...] -= rt[...]

    @pl.when(last)
    def _():
        @pl.loop(0, HOPS)
        def _(i):
            beside_own(i).wait_send()
            beside_other(i).wait_send()

        for i in (HOPS - 2, HOPS - 1):
            first_hop(0, i).wait_send()
            first_hop(1, i).wait_send()

        for i in range(4):
            for d in range(7):
                scatter(d, i).wait_send()

    @pl.when(jnp.logical_not(source_chip))
    def _():
        @pl.loop(0, HOPS)
        def _(i):
            share(i).wait_send()

            @pl.when(hops < 3)
            def _():
                forward(i).wait_send()

    @pl.when(lower)
    def _():
        for d in range(3):
            across(d).wait_send()

    @pl.when(taking & jnp.logical_not(last))
    def _():
        for i in range(CHUNKS - 4, CHUNKS):
            chunk(i).wait_send()

    @pl.when(chip_lower)
    def _():
        for d in range(3):
            spread(d).wait_send()


def copy_kernel(a, b, c, out_a, out_b, out_c):
    out_a[...], out_b[...], out_c[...] = a[...], b[...], c[...]


def shards(trail, fac, xf, lf, li, grad, cg, dg):
    dma = pltpu.SemaphoreType.DMA
    anywhere = pl.BlockSpec(memory_space=pl.ANY)
    vmem = pl.BlockSpec(memory_space=pltpu.VMEM)
    shape = jax.ShapeDtypeStruct
    square = (BLOCK, BLOCK)
    results = (
        shape((BLOCK, 128), F32), shape((64, BLOCK), F32), shape((2, 64, BLOCK), F32),
    )
    made = pl.pallas_call(
        kernel,
        name="adjoint",
        out_shape=results,
        in_specs=[anywhere] * 8,
        out_specs=[vmem] * 3,
        scratch_shapes=[
            pltpu.VMEM((BLOCK, 2048), BF16),
            pltpu.VMEM((2048, 1024), BF16),
            pltpu.VMEM((BLOCK, 1024), BF16),
            pltpu.VMEM(square, BF16),
            pltpu.VMEM((2, *square), BF16),
            pltpu.VMEM((2, *square), F32),
            pltpu.VMEM(square, BF16),
            pltpu.VMEM((2, *square), BF16),
            pltpu.VMEM((2048, BLOCK), BF16),
            pltpu.VMEM((2048, 1024), BF16),
            pltpu.VMEM((BLOCK, 1024), BF16),
            pltpu.VMEM((BLOCK, 1024), F32),
            pltpu.VMEM((BLOCK, 1024), F32),
            pltpu.VMEM((BLOCK, 1024), F32),
            pltpu.VMEM((6144, 128), F32),
            pltpu.VMEM((6144, 128), F32),
            pltpu.VMEM((3, 768, 128), F32),
            pltpu.VMEM((3, 192, 128), F32),
            pltpu.VMEM((7, 24, 128), F32),
            pltpu.VMEM((1024, 1024), BF16),
            pltpu.VMEM((1024, 1024), BF16),
            pltpu.VMEM((6, *square), BF16),
            pltpu.VMEM((3, *square), F32),
            pltpu.VMEM((2, 4, BLOCK, 128), F32),
            pltpu.VMEM((4, BLOCK, 128), F32),
            pltpu.VMEM((3, BLOCK, 128), F32),
            pltpu.VMEM((8, BLOCK, 128), F32),
            pltpu.VMEM((BLOCK, 128), F32),
            dma((10,)), dma((2, HOPS)), dma((HOPS,)), dma((2, HOPS)), dma((HOPS,)), dma((3,)), dma((3,)),
            dma((4,)), dma((4,)), dma((3,)), dma((3,)), dma((3,)), dma((3,)), dma((7,)), dma((7,)),
            dma((7,)), dma((7,)), dma((3,)), dma((3,)), dma((3,)), dma((3,)), dma((4,)), dma((4,)),
            dma((CHUNKS,)), dma((CHUNKS,)), dma, dma, dma((3,)), dma((3,)), dma((7, 4)), dma((4,)),
        ],
        compiler_params=pltpu.CompilerParams(
            collective_id=0, has_side_effects=True, vmem_limit_bytes=VMEM_BYTES
        ),
    )(trail, fac, xf, lf, li, grad, cg, dg)
    return pl.pallas_call(
        copy_kernel, name="results", out_shape=results, in_specs=[vmem] * 3, out_specs=[vmem] * 3
    )(*made)


def solution(mesh):
    fine = Mesh(mesh.devices.reshape(8, 4, 4, 2), ("z", "x", "y", "k"))
    row, col = ("z", "x"), ("y", "k")
    return jax.shard_map(
        shards,
        mesh=fine,
        in_specs=(P(row, col), P(col, None), P(), P(), P(), P(row, None), P(), P()),
        out_specs=(P(row, col), P(col, None), P(None, col, None)),
        check_vma=False,
    )
```

```python
import jax
import jax.numpy as jnp
from jax import lax
from jax.experimental import pallas as pl
from jax.experimental.pallas import tpu as pltpu
from jax.sharding import Mesh
from jax.sharding import PartitionSpec as P

MESH = pl.DeviceIdType.MESH
F32, BF16 = jnp.float32, jnp.bfloat16
BLOCK = 512
VMEM_BYTES = 62 * 1024 * 1024


def place():
    return tuple(lax.axis_index(a) for a in ("z", "x", "y", "k"))


def meet(peers):
    barrier = pltpu.get_barrier_semaphore()
    for peer in peers:
        pl.semaphore_signal(barrier, inc=1, device_id=peer, device_id_type=MESH)
    pl.semaphore_wait(barrier, len(peers))


def push(src, dst, send, recv, peer):
    return pltpu.make_async_remote_copy(
        src_ref=src, dst_ref=dst, send_sem=send, recv_sem=recv, device_id=peer, device_id_type=MESH
    )


def dot(a, b, ca=1, cb=0):
    return lax.dot_general(a, b, (((ca,), (cb,)), ((), ())), preferred_element_type=F32)


def split(a):
    high = a.astype(BF16)
    return high, (a - high.astype(F32)).astype(BF16)


def dot3(a, b, ca=1, cb=0):
    ah, al = a if isinstance(a, tuple) else split(a)
    bh, bl = b if isinstance(b, tuple) else split(b)
    return dot(ah, bh, ca, cb) + (dot(al, bh, ca, cb) + dot(ah, bl, ca, cb))


def dot2(a, b, ca=1, cb=0):
    if isinstance(a, tuple):
        return dot(a[0], b, ca, cb) + dot(a[1], b, ca, cb)
    return dot(a, b[0], ca, cb) + dot(a, b[1], ca, cb)


def symmetric(f):
    size = f.shape[0]
    rows = lax.broadcasted_iota(jnp.int32, (size, size), 0)
    cols = lax.broadcasted_iota(jnp.int32, (size, size), 1)
    halved = jnp.where(cols < rows, f, jnp.where(cols == rows, f * 0.5, 0.0))
    return halved + halved.T


def masked(m, row0, col0):
    rows = row0 + lax.broadcasted_iota(jnp.int32, m.shape, 0)
    cols = col0 + lax.broadcasted_iota(jnp.int32, m.shape, 1)
    scale = jnp.where(cols < rows, 1.0, jnp.where(cols == rows, 0.5, 0.0))
    return (m.astype(F32) * scale).astype(BF16)

CHUNKS = 32
SKEW = 4
LINES = BLOCK // CHUNKS
HOPS = 16


def kernel(
    trail, fac, xf, lf, li, grad, cg, dg,
    panel_out, cross_out, diag_out,
    m, fv, gv, xv, lfv, liv, cgv, dgv,
    mx, fz, f, mf, t, arrived, w, full, r1, r2, r3,
    ph, plo, pairs, consts, yp, q0, q1, tq, rt,
    ls, fs, fr, hs, hr, xs, xr,
    s0, v0, s1, v1, s2, v2, s3, v3, g3, u3, g2, u2, g1, u1, g0, u0,
    ts, tr, a0, b0, a1, b1s, es, er,
):
    z, x, y, k = place()
    c = 2 * y + k
    ys, ks = z >> 1, z & 1
    sibling = (z, x, y, 1 - k)
    lower = c <= z
    last = c == z
    chip_lower = 2 * y <= z
    source_chip = y == ys
    yn = (lax.rem(y + 3, 4), lax.rem(y + 1, 4))
    px = [lax.rem(x + d, 4) for d in (1, 2, 3)]
    py = [lax.rem(y + d, 4) for d in (1, 2, 3)]
    pz = [lax.rem(z + d, 8) for d in range(1, 8)]
    pc = [lax.rem(c + d, 8) for d in range(1, 8)]
    mine = pl.ds(pl.multiple_of(x * BLOCK, BLOCK), BLOCK)

    def local(n, src, dst):
        return pltpu.make_async_copy(src, dst, ls.at[n])

    get_trail = local(0, trail, m)
    get_factor = local(1, fac, fv)
    get_grad = local(2, grad, gv)
    get_small = [
        local(3, xf, xv), local(4, lf, lfv), local(5, li, liv), local(6, cg, cgv), local(7, dg, dgv)
    ]
    get_own = local(8, trail.at[:, mine], mx.at[mine, :])
    get_source = local(9, fac, fz)

    @pl.when(lower)
    def _():
        get_trail.start()
        get_factor.start()
        get_own.start()

    get_grad.start()
    for copy in get_small:
        copy.start()

    @pl.when(last)
    def _():
        get_source.start()

    meet(
        [(z, p, y, k) for p in px]
        + [(z, x, p >> 1, p & 1) for p in pc]
        + [(p, x, y, k) for p in pz]
    )

    def rows(s, i):
        block = lax.rem(x + i // 4, 4)
        return pl.ds(pl.multiple_of(block * BLOCK + s * 256 + lax.rem(i, 4) * 64, 64), 64)

    def first_hop(s, i):
        return push(
            fac.at[rows(s, i), :], fz.at[rows(s, i), :], fs.at[s, i], fr.at[i], (z, x, yn[s], s)
        )

    def beside_own(i):
        return push(fac.at[rows(1 - k, i), :], fz.at[rows(1 - k, i), :], hs.at[0, i], fr.at[i], sibling)

    def beside_other(i):
        return push(fac.at[rows(k, i), :], fz.at[rows(k, i), :], hs.at[1, i], hr.at[i], sibling)

    onward_y = jnp.where(k == 0, yn[0], yn[1])
    hops = jnp.where(k == 0, (ys - y + 4) & 3, (y - ys + 4) & 3)

    def forward(i):
        return push(
            fz.at[rows(k, i), :], fz.at[rows(k, i), :], fs.at[0, i], fr.at[i], (z, x, onward_y, k)
        )

    def share(i):
        return push(fz.at[rows(k, i), :], fz.at[rows(k, i), :], hs.at[0, i], hr.at[i], sibling)

    def other(i):
        return push(fz.at[rows(1 - k, i), :], fz.at[rows(1 - k, i), :], hs.at[0, i], hr.at[i], sibling)

    def across(d):
        return push(
            trail.at[:, pl.ds(pl.multiple_of(px[d] * BLOCK, 128), BLOCK)],
            mx.at[mine, :],
            xs.at[d],
            xr.at[d],
            (z, px[d], y, k),
        )

    def feed(lo, hi):
        if lo >= HOPS:
            return

        @pl.when(last)
        def _():
            @pl.loop(lo, min(hi, HOPS))
            def _(i):
                @pl.when(i >= 2)
                def _():
                    first_hop(0, i - 2).wait_send()
                    first_hop(1, i - 2).wait_send()

                first_hop(0, i).start()
                first_hop(1, i).start()
                beside_own(i).start()
                beside_other(i).start()

    feed(0, 2)

    @pl.when(lower)
    def _():
        for d in (2, 1, 0):
            across(d).start()

    def relays(lo, hi):
        feed(lo + 2, hi + 2)

        @pl.when(jnp.logical_not(source_chip))
        def _():
            @pl.loop(lo, hi)
            def _(i):
                forward(i).wait_recv()

                @pl.when(hops < 3)
                def _():
                    forward(i).start()

                share(i).start()

        @pl.when(source_chip & (k != ks))
        def _():
            @pl.loop(lo, hi)
            def _(i):
                forward(i).wait_recv()

    def others(lo, hi):
        @pl.when(jnp.logical_not(last))
        def _():
            @pl.loop(lo, hi)
            def _(i):
                other(i).wait_recv()

    @pl.when(lower)
    def _():
        get_trail.wait()
        get_factor.wait()

    def product(i):
        @pl.when(lower)
        def _():
            here = slice(i * 128, (i + 1) * 128)

            @pl.when(last)
            def _():
                m[here, :] = masked(m[here, :], x * BLOCK + i * 128, 0)

            mf[here, :] = dot(m[here, :], fv[...])

    @pl.when(c > z)
    def _():
        mf[...] = jnp.zeros_like(mf)
        w[...] = jnp.zeros_like(w)
        t[...] = jnp.zeros_like(t)

    for i in range(4):
        relays(i, i + 1)
        product(i)

    get_grad.wait()

    @pl.when(last)
    def _():
        get_source.wait()

    own = jnp.where(last, 1.0, 0.0)

    def add_block(block, a, b):
        @pl.when(lower)
        def _():
            mfa = mf[:, a * BLOCK : (a + 1) * BLOCK]
            mfb = mf[:, b * BLOCK : (b + 1) * BLOCK]
            ga = gv[:, a * BLOCK : (a + 1) * BLOCK].astype(F32) * own
            fa = f[:, a * BLOCK : (a + 1) * BLOCK]
            fb = f[:, b * BLOCK : (b + 1) * BLOCK]
            value = dot2(split(ga - mfa), fb, 0, 0) - dot2(fa, split(mfb), 0, 0)
            for j in range(4):
                w[pl.ds(j * 1536 + block * BLOCK, BLOCK), :] = value[:, j * 128 : (j + 1) * 128]

    half = k * 3072
    first = jnp.where(k == 0, y, x)
    second = jnp.where(k == 0, x, y)
    p1 = [lax.rem(first + d, 4) for d in (1, 2, 3)]
    p2 = [lax.rem(second + d, 4) for d in (1, 2, 3)]
    at1 = half + first * 768
    at2 = at1 + second * 192
    at3 = at2 + z * 24

    def part(at, n):
        return pl.ds(pl.multiple_of(at, 8), n)

    def along_first(p):
        return (z, jnp.where(k == 0, x, p), jnp.where(k == 0, p, y), k)

    def along_second(p):
        return (z, jnp.where(k == 0, p, x), jnp.where(k == 0, y, p), k)

    def out1(d):
        return push(w.at[part(half + p1[d] * 768, 768), :], r1.at[d], s1.at[d], v1.at[d], along_first(p1[d]))

    def out2(d):
        return push(w.at[part(at1 + p2[d] * 192, 192), :], r2.at[d], s2.at[d], v2.at[d], along_second(p2[d]))

    def out3(d):
        return push(w.at[part(at2 + pz[d] * 24, 24), :], r3.at[d], s3.at[d], v3.at[d], (pz[d], x, y, k))

    def whole(at, n, send, recv, peer):
        return push(full.at[part(at, n), :], full.at[part(at, n), :], send, recv, peer)

    def start(copies):
        for copy in copies:
            copy.start()

    def finish(copies):
        for copy in copies:
            copy.wait()

    def quarter(at, j):
        return part(at + lax.rem(j, 4) * 768, 768)

    def swapped(j):
        away = quarter(3072 - half, second + 1 + j)
        return push(w.at[away, :], full.at[away, :], s0.at[j], v0.at[j], sibling)

    c0 = [swapped(j) for j in range(4)]
    c1 = [out1(d) for d in range(3)]
    c2 = [out2(d) for d in range(3)]
    c3 = [out3(d) for d in range(7)]
    c4 = [whole(at3, 24, g3.at[d], u3.at[d], (pz[d], x, y, k)) for d in range(7)]
    c5 = [whole(at2, 192, g2.at[d], u2.at[d], along_second(p2[d])) for d in range(3)]
    c6 = [whole(at1, 768, g1.at[d], u1.at[d], along_first(p1[d])) for d in range(3)]
    c7 = [
        whole(half + lax.rem(first + 4 - j, 4) * 768, 768, g0.at[j], u0.at[j], sibling) for j in range(4)
    ]
    def sum_one():
        finish(c1)
        w[part(at1, 768), :] += r1[0] + r1[1] + r1[2]
        start(c2)

    def pre_one():
        finish(get_small)
        ph[0:BLOCK, 0:BLOCK], plo[0:BLOCK, 0:BLOCK] = split(liv[0])
        ph[BLOCK:, BLOCK:], plo[BLOCK:, BLOCK:] = split(liv[1])
        ph[0:BLOCK, BLOCK:] = jnp.zeros((BLOCK, BLOCK), BF16)
        plo[0:BLOCK, BLOCK:] = jnp.zeros((BLOCK, BLOCK), BF16)

    def li0():
        return ph[0:BLOCK, 0:BLOCK], plo[0:BLOCK, 0:BLOCK]

    def li1():
        return ph[BLOCK:, BLOCK:], plo[BLOCK:, BLOCK:]

    def minus_b1():
        return ph[BLOCK:, 0:BLOCK], plo[BLOCK:, 0:BLOCK]

    def pair(n):
        return pairs[2 * n], pairs[2 * n + 1]

    def keep(n, value):
        pairs[2 * n], pairs[2 * n + 1] = split(value)

    def pre_cross():
        keep(0, dot2(li1(), xv[...]))

    def pre_b1():
        high, low = split(dot3(pair(0), li0()))
        ph[BLOCK:, 0:BLOCK], plo[BLOCK:, 0:BLOCK] = -high, -low

    def pre_j0():
        keep(0, dot2(li0(), lfv[0]))

    def pre_j1():
        keep(1, dot2(li1(), lfv[1]))

    def pre_b2():
        keep(2, -dot2(minus_b1(), lfv[0]))

    def pre_three():
        consts[0] = dot(lfv[0], dgv[0], 0, 0)
        consts[1] = dot(lfv[1], dgv[1], 0, 0)
        consts[2] = dot2(cgv[...], pair(0))

    def transposed(j):
        @pl.when(lower)
        def _():
            if j == 0:
                get_own.wait()
            else:
                across(3 - j).wait_recv()
            block = lax.rem(x + j, 4)
            here = pl.ds(pl.multiple_of(block * BLOCK, BLOCK), BLOCK)

            @pl.when(last)
            def _():
                mx[here, :] = masked(mx[here, :], block * BLOCK, x * BLOCK)

            @pl.loop(0, 2)
            def _(i):
                lines = pl.ds(pl.multiple_of(i * 256, 256), 256)
                value = dot(mx[here, lines], fz[here, :], 0, 0)
                if j == 0:
                    t[lines, :] = value
                else:
                    t[lines, :] += value

    def ready():
        others(0, 4)

        @pl.when(lower)
        def _():
            f[...] = fz[mine, :]

    def pass_on(j):
        c0[j].wait_recv()
        here = quarter(half, first + 1 + j)
        w[here, :] += full[here, :]
        if j < 3:
            c1[j].start()

    between = {
        7: [ready, lambda: add_block(0, 1, 1)],
        8: [lambda: add_block(1, 1, 0)],
        9: [lambda: add_block(2, 0, 0), lambda: start(c0)],
        10: [pre_one],
        11: [lambda: pass_on(0), lambda: pass_on(1)],
        12: [lambda: pass_on(2), lambda: pass_on(3), pre_cross],
        13: [lambda: others(4, 8), pre_b1],
        14: [lambda: transposed(0)],
    }
    for i in range(4, HOPS):
        relays(i, i + 1)
        for piece in between.get(i, []):
            piece()
    transposed(1)
    others(8, 12)
    transposed(2)
    others(12, 16)
    transposed(3)

    before, after = lax.rem(z + 7, 8), lax.rem(z + 1, 8)
    position = jnp.where(k == 0, 7 - z, (z - c + 7) & 7)
    taking = (k == 1) | lower
    onward_z = jnp.where(k == 0, before, after)

    def chunk(i):
        here = pl.ds(pl.multiple_of(i * LINES, LINES), LINES)
        return push(t.at[here, :], arrived.at[here, :], ts.at[i], tr.at[i], (onward_z, x, y, k))

    def mapped(part_rows, store):
        h, l = split(part_rows)
        low = dot3((h, l), (ph[:, :BLOCK], plo[:, :BLOCK]))
        high = dot3((h[:, BLOCK:], l[:, BLOCK:]), (ph[BLOCK:, BLOCK:], plo[BLOCK:, BLOCK:]))
        for g in range(4):
            store(g, low[:, g * 128 : (g + 1) * 128])
            store(g + 4, high[:, g * 128 : (g + 1) * 128])

    def direct(i):
        @pl.when(chip_lower)
        def _():
            here = slice(i * 128, (i + 1) * 128)

            def store(g, value):
                yp[g % 2, g // 2, here, :] = value

            mapped(mf[here, :], store)

    swap = push(yp.at[1 - k], q0, a0, b0, sibling)

    def spread(d):
        return push(yp.at[k, py[d]], q1.at[d], a1.at[d], b1s.at[d], (z, x, py[d], k))

    def swap_start():
        @pl.when(chip_lower)
        def _():
            swap.start()

    def swap_end():
        @pl.when(chip_lower)
        def _():
            swap.wait()
            yp[pl.ds(k, 1)] += q0[...][None]
            for d in range(3):
                spread(d).start()

    def scatter(d, i):
        here = pl.ds(pl.multiple_of(i * 128, 128), 128)
        to = pc[d]
        return push(tq.at[to, here, :], rt.at[here, :], es.at[d, i], er.at[i], (z, x, to >> 1, to & 1))

    def last_part(i):
        here = pl.ds(pl.multiple_of(i * 128, 128), 128)

        def store(g, value):
            tq[g, here, :] = value

        mapped(t[here, :], store)
        for d in range(7):
            scatter(d, i).start()

    def chain(s):
        i = s - SKEW * position

        @pl.when(taking & (i >= 0) & (i < CHUNKS))
        def _():
            here = pl.ds(pl.multiple_of(i * LINES, LINES), LINES)

            @pl.when(position > 0)
            def _():
                chunk(i).wait_recv()
                t[here, :] += arrived[here, :]

            @pl.when(jnp.logical_not(last))
            def _():
                @pl.when(i >= 4)
                def _():
                    chunk(i - 4).wait_send()

                chunk(i).start()

            @pl.when(last & (lax.rem(i, 8) == 7))
            def _():
                last_part(i >> 3)

    def sum_two():
        finish(c2)
        w[part(at2, 192), :] += r2[0] + r2[1] + r2[2]
        start(c3)

    def sum_three():
        finish(c3)
        full[part(at3, 24), :] = w[part(at3, 24), :] + (
            ((r3[0] + r3[1]) + (r3[2] + r3[3])) + ((r3[4] + r3[5]) + r3[6])
        )
        start(c4)

    def then(done, go):
        def run():
            finish(done)
            start(go)

        return run

    def gather_one():
        finish(c5)
        start(c6)
        c7[0].start()

    def gather_two():
        for d in range(3):
            c6[d].wait_recv()
            c7[d + 1].start()

    def square(n):
        return pl.ds(n // 2 * BLOCK, BLOCK), pl.ds(n % 2 * BLOCK, BLOCK)

    def hold(n, value):
        fv[square(2 * n)], fv[square(2 * n + 1)] = split(value)

    def held(n):
        return fv[square(2 * n)], fv[square(2 * n + 1)]

    def total(block):
        return jnp.concatenate(
            [full[pl.ds(j * 1536 + block * BLOCK, BLOCK), :] for j in range(4)], axis=1
        )

    slab = pl.ds(pl.multiple_of(c * 64, 64), 64)

    def turned(parts):
        pick = jnp.where(
            lax.broadcasted_iota(jnp.int32, (BLOCK, 64), 0)
            == c * 64 + lax.broadcasted_iota(jnp.int32, (BLOCK, 64), 1),
            1.0,
            0.0,
        ).astype(BF16)
        return tuple(dot(pick, part_of, 0, 1).astype(BF16) for part_of in parts)

    def dense_one():
        hold(0, symmetric(consts[1] - dot3(pair(1), split(total(0)), 0, 0)))

    def dense_two():
        hold(1, total(1))
        mf[:, 0:BLOCK] = dot3(held(1), pair(0))

    def dense_three():
        hold(2, mf[:, 0:BLOCK] + dot3(held(0), pair(2)))

    def dense_four():
        hold(3, consts[2] - dot3(li1(), held(2), 0, 0))

    def dense_five():
        mf[:, BLOCK:] = consts[0] - dot3(pair(0), split(total(2)), 0, 0)

    def dense_six():
        mf[:, BLOCK:] += dot3(pair(2), held(1), 0, 0)

    def dense_seven():
        hold(2, symmetric(mf[:, BLOCK:] - dot2(held(3), xv[...], 0, 0)))

    def dense_eight():
        lit1 = turned(li1())
        ls1 = split(dot3(lit1, held(0)))
        diag_out[1] = dot3(ls1, li1())
        cross_out[...] = dot2(cgv[slab, :], li0()) - (
            dot3(split(dot3(lit1, held(1))), li0()) - dot3(ls1, minus_b1())
        )

    def dense_nine():
        diag_out[0] = dot3(split(dot3(turned(li0()), held(2))), li0())

    cols = pl.ds(pl.multiple_of(c * 128, 128), 128)

    def own_gradient():
        panel_out[...] = dot2(gv[...], (ph[:, cols], plo[:, cols]))

    beside = {
        1: sum_one,
        2: lambda: direct(0),
        4: lambda: direct(1),
        7: sum_two,
        8: lambda: direct(2),
        10: lambda: direct(3),
        11: swap_start,
        13: sum_three,
        15: pre_j0,
        17: pre_j1,
        19: then(c4, c5),
        21: pre_b2,
        23: swap_end,
        25: gather_one,
        29: pre_three,
        33: own_gradient,
        41: gather_two,
    }

    @pl.loop(0, CHUNKS + 7 * SKEW)
    def _(s):
        chain(s)
        for at, step in beside.items():
            pl.when(s == at)(step)

    for copy in c0 + c6:
        copy.wait_send()
    finish(c7)
    for step in (
        dense_one, dense_two, dense_three, dense_four, dense_five, dense_six, dense_seven,
        dense_eight, dense_nine,
    ):
        step()
    @pl.when(chip_lower)
    def _():
        panel_out[...] -= yp[k, y]

    for d in range(3):
        @pl.when(2 * lax.rem(y + 3 - d, 4) <= z)
        def _():
            spread(d).wait_recv()
            panel_out[...] -= q1[d]

    @pl.when(last)
    def _():
        panel_out[...] -= tq[c]

    @pl.when(jnp.logical_not(last))
    def _():
        for i in range(4):
            scatter(0, i).wait_recv()
        panel_out[...] -= rt[...]

    @pl.when(last)
    def _():
        @pl.loop(0, HOPS)
        def _(i):
            beside_own(i).wait_send()
            beside_other(i).wait_send()

        for i in (HOPS - 2, HOPS - 1):
            first_hop(0, i).wait_send()
            first_hop(1, i).wait_send()

        for i in range(4):
            for d in range(7):
                scatter(d, i).wait_send()

    @pl.when(jnp.logical_not(source_chip))
    def _():
        @pl.loop(0, HOPS)
        def _(i):
            share(i).wait_send()

            @pl.when(hops < 3)
            def _():
                forward(i).wait_send()

    @pl.when(lower)
    def _():
        for d in range(3):
            across(d).wait_send()

    @pl.when(taking & jnp.logical_not(last))
    def _():
        for i in range(CHUNKS - 4, CHUNKS):
            chunk(i).wait_send()

    @pl.when(chip_lower)
    def _():
        for d in range(3):
            spread(d).wait_send()


def copy_kernel(a, b, c, out_a, out_b, out_c):
    out_a[...], out_b[...], out_c[...] = a[...], b[...], c[...]


def shards(trail, fac, xf, lf, li, grad, cg, dg):
    dma = pltpu.SemaphoreType.DMA
    anywhere = pl.BlockSpec(memory_space=pl.ANY)
    vmem = pl.BlockSpec(memory_space=pltpu.VMEM)
    shape = jax.ShapeDtypeStruct
    square = (BLOCK, BLOCK)
    results = (
        shape((BLOCK, 128), F32), shape((64, BLOCK), F32), shape((2, 64, BLOCK), F32),
    )
    made = pl.pallas_call(
        kernel,
        name="adjoint",
        out_shape=results,
        in_specs=[anywhere] * 8,
        out_specs=[vmem] * 3,
        scratch_shapes=[
            pltpu.VMEM((BLOCK, 2048), BF16),
            pltpu.VMEM((2048, 1024), BF16),
            pltpu.VMEM((BLOCK, 1024), BF16),
            pltpu.VMEM(square, BF16),
            pltpu.VMEM((2, *square), BF16),
            pltpu.VMEM((2, *square), F32),
            pltpu.VMEM(square, BF16),
            pltpu.VMEM((2, *square), BF16),
            pltpu.VMEM((2048, BLOCK), BF16),
            pltpu.VMEM((2048, 1024), BF16),
            pltpu.VMEM((BLOCK, 1024), BF16),
            pltpu.VMEM((BLOCK, 1024), F32),
            pltpu.VMEM((BLOCK, 1024), F32),
            pltpu.VMEM((BLOCK, 1024), F32),
            pltpu.VMEM((6144, 128), F32),
            pltpu.VMEM((6144, 128), F32),
            pltpu.VMEM((3, 768, 128), F32),
            pltpu.VMEM((3, 192, 128), F32),
            pltpu.VMEM((7, 24, 128), F32),
            pltpu.VMEM((1024, 1024), BF16),
            pltpu.VMEM((1024, 1024), BF16),
            pltpu.VMEM((6, *square), BF16),
            pltpu.VMEM((3, *square), F32),
            pltpu.VMEM((2, 4, BLOCK, 128), F32),
            pltpu.VMEM((4, BLOCK, 128), F32),
            pltpu.VMEM((3, BLOCK, 128), F32),
            pltpu.VMEM((8, BLOCK, 128), F32),
            pltpu.VMEM((BLOCK, 128), F32),
            dma((10,)), dma((2, HOPS)), dma((HOPS,)), dma((2, HOPS)), dma((HOPS,)), dma((3,)), dma((3,)),
            dma((4,)), dma((4,)), dma((3,)), dma((3,)), dma((3,)), dma((3,)), dma((7,)), dma((7,)),
            dma((7,)), dma((7,)), dma((3,)), dma((3,)), dma((3,)), dma((3,)), dma((4,)), dma((4,)),
            dma((CHUNKS,)), dma((CHUNKS,)), dma, dma, dma((3,)), dma((3,)), dma((7, 4)), dma((4,)),
        ],
        compiler_params=pltpu.CompilerParams(
            collective_id=0, has_side_effects=True, vmem_limit_bytes=VMEM_BYTES
        ),
    )(trail, fac, xf, lf, li, grad, cg, dg)
    return pl.pallas_call(
        copy_kernel, name="results", out_shape=results, in_specs=[vmem] * 3, out_specs=[vmem] * 3
    )(*made)


def solution(mesh):
    fine = Mesh(mesh.devices.reshape(8, 4, 4, 2), ("z", "x", "y", "k"))
    row, col = ("z", "x"), ("y", "k")
    return jax.shard_map(
        shards,
        mesh=fine,
        in_specs=(P(row, col), P(col, None), P(), P(), P(), P(row, None), P(), P()),
        out_specs=(P(row, col), P(col, None), P(None, col, None)),
        check_vma=False,
    )
```

```python
import jax
import jax.numpy as jnp
from jax import lax
from jax.experimental import pallas as pl
from jax.experimental.pallas import tpu as pltpu
from jax.sharding import Mesh
from jax.sharding import PartitionSpec as P

MESH = pl.DeviceIdType.MESH
F32, BF16 = jnp.float32, jnp.bfloat16
BLOCK = 512
VMEM_BYTES = 62 * 1024 * 1024


def place():
    return tuple(lax.axis_index(a) for a in ("z", "x", "y", "k"))


def meet(peers):
    barrier = pltpu.get_barrier_semaphore()
    for peer in peers:
        pl.semaphore_signal(barrier, inc=1, device_id=peer, device_id_type=MESH)
    pl.semaphore_wait(barrier, len(peers))


def push(src, dst, send, recv, peer):
    return pltpu.make_async_remote_copy(
        src_ref=src, dst_ref=dst, send_sem=send, recv_sem=recv, device_id=peer, device_id_type=MESH
    )


def dot(a, b, ca=1, cb=0):
    return lax.dot_general(a, b, (((ca,), (cb,)), ((), ())), preferred_element_type=F32)


def split(a):
    high = a.astype(BF16)
    return high, (a - high.astype(F32)).astype(BF16)


def dot3(a, b, ca=1, cb=0):
    ah, al = a if isinstance(a, tuple) else split(a)
    bh, bl = b if isinstance(b, tuple) else split(b)
    return dot(ah, bh, ca, cb) + (dot(al, bh, ca, cb) + dot(ah, bl, ca, cb))


def dot2(a, b, ca=1, cb=0):
    if isinstance(a, tuple):
        return dot(a[0], b, ca, cb) + dot(a[1], b, ca, cb)
    return dot(a, b[0], ca, cb) + dot(a, b[1], ca, cb)


def symmetric(f):
    size = f.shape[0]
    rows = lax.broadcasted_iota(jnp.int32, (size, size), 0)
    cols = lax.broadcasted_iota(jnp.int32, (size, size), 1)
    halved = jnp.where(cols < rows, f, jnp.where(cols == rows, f * 0.5, 0.0))
    return halved + halved.T


def masked(m, row0, col0):
    rows = row0 + lax.broadcasted_iota(jnp.int32, m.shape, 0)
    cols = col0 + lax.broadcasted_iota(jnp.int32, m.shape, 1)
    scale = jnp.where(cols < rows, 1.0, jnp.where(cols == rows, 0.5, 0.0))
    return (m.astype(F32) * scale).astype(BF16)

CHUNKS = 32
SKEW = 4
LINES = BLOCK // CHUNKS
HOPS = 16


def kernel(
    trail, fac, xf, lf, li, grad, cg, dg,
    panel_out, cross_out, diag_out,
    m, fv, gv, xv, lfv, liv, cgv, dgv,
    mx, fz, f, mf, t, arrived, w, full, r1, r2, r3,
    ph, plo, pairs, consts, yp, q0, q1, tq, rt,
    ls, fs, fr, hs, hr, xs, xr,
    s0, v0, s1, v1, s2, v2, s3, v3, g3, u3, g2, u2, g1, u1, g0, u0,
    ts, tr, a0, b0, a1, b1s, es, er,
):
    z, x, y, k = place()
    c = 2 * y + k
    ys, ks = z >> 1, z & 1
    sibling = (z, x, y, 1 - k)
    lower = c <= z
    last = c == z
    chip_lower = 2 * y <= z
    source_chip = y == ys
    yn = (lax.rem(y + 3, 4), lax.rem(y + 1, 4))
    px = [lax.rem(x + d, 4) for d in (1, 2, 3)]
    py = [lax.rem(y + d, 4) for d in (1, 2, 3)]
    pz = [lax.rem(z + d, 8) for d in range(1, 8)]
    pc = [lax.rem(c + d, 8) for d in range(1, 8)]
    mine = pl.ds(pl.multiple_of(x * BLOCK, BLOCK), BLOCK)

    def local(n, src, dst):
        return pltpu.make_async_copy(src, dst, ls.at[n])

    get_trail = local(0, trail, m)
    get_factor = local(1, fac, fv)
    get_grad = local(2, grad, gv)
    get_small = [
        local(3, xf, xv), local(4, lf, lfv), local(5, li, liv), local(6, cg, cgv), local(7, dg, dgv)
    ]
    get_own = local(8, trail.at[:, mine], mx.at[mine, :])
    get_source = local(9, fac, fz)

    @pl.when(lower)
    def _():
        get_trail.start()
        get_factor.start()
        get_own.start()

    get_grad.start()
    for copy in get_small:
        copy.start()

    @pl.when(last)
    def _():
        get_source.start()

    meet(
        [(z, p, y, k) for p in px]
        + [(z, x, p >> 1, p & 1) for p in pc]
        + [(p, x, y, k) for p in pz]
    )

    def rows(s, i):
        block = lax.rem(x + i // 4, 4)
        return pl.ds(pl.multiple_of(block * BLOCK + s * 256 + lax.rem(i, 4) * 64, 64), 64)

    def first_hop(s, i):
        return push(
            fac.at[rows(s, i), :], fz.at[rows(s, i), :], fs.at[s, i], fr.at[i], (z, x, yn[s], s)
        )

    def beside_own(i):
        return push(fac.at[rows(1 - k, i), :], fz.at[rows(1 - k, i), :], hs.at[0, i], fr.at[i], sibling)

    def beside_other(i):
        return push(fac.at[rows(k, i), :], fz.at[rows(k, i), :], hs.at[1, i], hr.at[i], sibling)

    onward_y = jnp.where(k == 0, yn[0], yn[1])
    hops = jnp.where(k == 0, (ys - y + 4) & 3, (y - ys + 4) & 3)

    def forward(i):
        return push(
            fz.at[rows(k, i), :], fz.at[rows(k, i), :], fs.at[0, i], fr.at[i], (z, x, onward_y, k)
        )

    def share(i):
        return push(fz.at[rows(k, i), :], fz.at[rows(k, i), :], hs.at[0, i], hr.at[i], sibling)

    def other(i):
        return push(fz.at[rows(1 - k, i), :], fz.at[rows(1 - k, i), :], hs.at[0, i], hr.at[i], sibling)

    def across(d):
        return push(
            trail.at[:, pl.ds(pl.multiple_of(px[d] * BLOCK, 128), BLOCK)],
            mx.at[mine, :],
            xs.at[d],
            xr.at[d],
            (z, px[d], y, k),
        )

    def feed(lo, hi):
        if lo >= HOPS:
            return

        @pl.when(last)
        def _():
            @pl.loop(lo, min(hi, HOPS))
            def _(i):
                @pl.when(i >= 2)
                def _():
                    first_hop(0, i - 2).wait_send()
                    first_hop(1, i - 2).wait_send()

                first_hop(0, i).start()
                first_hop(1, i).start()
                beside_own(i).start()
                beside_other(i).start()

    feed(0, 2)

    @pl.when(lower)
    def _():
        for d in (2, 1, 0):
            across(d).start()

    def relays(lo, hi):
        feed(lo + 2, hi + 2)

        @pl.when(jnp.logical_not(source_chip))
        def _():
            @pl.loop(lo, hi)
            def _(i):
                forward(i).wait_recv()

                @pl.when(hops < 3)
                def _():
                    forward(i).start()

                share(i).start()

        @pl.when(source_chip & (k != ks))
        def _():
            @pl.loop(lo, hi)
            def _(i):
                forward(i).wait_recv()

    def others(lo, hi):
        @pl.when(jnp.logical_not(last))
        def _():
            @pl.loop(lo, hi)
            def _(i):
                other(i).wait_recv()

    @pl.when(lower)
    def _():
        get_trail.wait()
        get_factor.wait()

    def product(i):
        @pl.when(lower)
        def _():
            here = slice(i * 128, (i + 1) * 128)

            @pl.when(last)
            def _():
                m[here, :] = masked(m[here, :], x * BLOCK + i * 128, 0)

            mf[here, :] = dot(m[here, :], fv[...])

    @pl.when(c > z)
    def _():
        mf[...] = jnp.zeros_like(mf)
        w[...] = jnp.zeros_like(w)
        t[...] = jnp.zeros_like(t)

    for i in range(4):
        relays(i, i + 1)
        product(i)

    get_grad.wait()

    @pl.when(last)
    def _():
        get_source.wait()

    own = jnp.where(last, 1.0, 0.0)

    def add_block(block, a, b):
        @pl.when(lower)
        def _():
            mfa = mf[:, a * BLOCK : (a + 1) * BLOCK]
            mfb = mf[:, b * BLOCK : (b + 1) * BLOCK]
            ga = gv[:, a * BLOCK : (a + 1) * BLOCK].astype(F32) * own
            fa = f[:, a * BLOCK : (a + 1) * BLOCK]
            fb = f[:, b * BLOCK : (b + 1) * BLOCK]
            value = dot2(split(ga - mfa), fb, 0, 0) - dot2(fa, split(mfb), 0, 0)
            for j in range(4):
                w[pl.ds(j * 1536 + block * BLOCK, BLOCK), :] = value[:, j * 128 : (j + 1) * 128]

    half = k * 3072
    first = jnp.where(k == 0, y, x)
    second = jnp.where(k == 0, x, y)
    p1 = [lax.rem(first + d, 4) for d in (1, 2, 3)]
    p2 = [lax.rem(second + d, 4) for d in (1, 2, 3)]
    at1 = half + first * 768
    at2 = at1 + second * 192
    at3 = at2 + z * 24

    def part(at, n):
        return pl.ds(pl.multiple_of(at, 8), n)

    def along_first(p):
        return (z, jnp.where(k == 0, x, p), jnp.where(k == 0, p, y), k)

    def along_second(p):
        return (z, jnp.where(k == 0, p, x), jnp.where(k == 0, y, p), k)

    def out1(d):
        return push(w.at[part(half + p1[d] * 768, 768), :], r1.at[d], s1.at[d], v1.at[d], along_first(p1[d]))

    def out2(d):
        return push(w.at[part(at1 + p2[d] * 192, 192), :], r2.at[d], s2.at[d], v2.at[d], along_second(p2[d]))

    def out3(d):
        return push(w.at[part(at2 + pz[d] * 24, 24), :], r3.at[d], s3.at[d], v3.at[d], (pz[d], x, y, k))

    def whole(at, n, send, recv, peer):
        return push(full.at[part(at, n), :], full.at[part(at, n), :], send, recv, peer)

    def start(copies):
        for copy in copies:
            copy.start()

    def finish(copies):
        for copy in copies:
            copy.wait()

    def quarter(at, j):
        return part(at + lax.rem(j, 4) * 768, 768)

    def swapped(j):
        away = quarter(3072 - half, second + 1 + j)
        return push(w.at[away, :], full.at[away, :], s0.at[j], v0.at[j], sibling)

    c0 = [swapped(j) for j in range(4)]
    c1 = [out1(d) for d in range(3)]
    c2 = [out2(d) for d in range(3)]
    c3 = [out3(d) for d in range(7)]
    c4 = [whole(at3, 24, g3.at[d], u3.at[d], (pz[d], x, y, k)) for d in range(7)]
    c5 = [whole(at2, 192, g2.at[d], u2.at[d], along_second(p2[d])) for d in range(3)]
    c6 = [whole(at1, 768, g1.at[d], u1.at[d], along_first(p1[d])) for d in range(3)]
    c7 = [
        whole(half + lax.rem(first + 4 - j, 4) * 768, 768, g0.at[j], u0.at[j], sibling) for j in range(4)
    ]
    def pre_one():
        finish(get_small)
        ph[0:BLOCK, 0:BLOCK], plo[0:BLOCK, 0:BLOCK] = split(liv[0])
        ph[BLOCK:, BLOCK:], plo[BLOCK:, BLOCK:] = split(liv[1])
        ph[0:BLOCK, BLOCK:] = jnp.zeros((BLOCK, BLOCK), BF16)
        plo[0:BLOCK, BLOCK:] = jnp.zeros((BLOCK, BLOCK), BF16)

    def li0():
        return ph[0:BLOCK, 0:BLOCK], plo[0:BLOCK, 0:BLOCK]

    def li1():
        return ph[BLOCK:, BLOCK:], plo[BLOCK:, BLOCK:]

    def minus_b1():
        return ph[BLOCK:, 0:BLOCK], plo[BLOCK:, 0:BLOCK]

    def pair(n):
        return pairs[2 * n], pairs[2 * n + 1]

    def keep(n, value):
        pairs[2 * n], pairs[2 * n + 1] = split(value)

    def pre_cross():
        keep(0, dot2(li1(), xv[...]))

    def pre_b1():
        high, low = split(dot3(pair(0), li0()))
        ph[BLOCK:, 0:BLOCK], plo[BLOCK:, 0:BLOCK] = -high, -low

    def pre_j0():
        keep(0, dot2(li0(), lfv[0]))

    def pre_j1():
        keep(1, dot2(li1(), lfv[1]))

    def pre_b2():
        keep(2, -dot2(minus_b1(), lfv[0]))

    def pre_three():
        consts[0] = dot(lfv[0], dgv[0], 0, 0)
        consts[1] = dot(lfv[1], dgv[1], 0, 0)
        consts[2] = dot2(cgv[...], pair(0))

    def transposed(j):
        @pl.when(lower)
        def _():
            if j == 0:
                get_own.wait()
            else:
                across(3 - j).wait_recv()
            block = lax.rem(x + j, 4)
            here = pl.ds(pl.multiple_of(block * BLOCK, BLOCK), BLOCK)

            @pl.when(last)
            def _():
                mx[here, :] = masked(mx[here, :], block * BLOCK, x * BLOCK)

            @pl.loop(0, 2)
            def _(i):
                lines = pl.ds(pl.multiple_of(i * 256, 256), 256)
                value = dot(mx[here, lines], fz[here, :], 0, 0)
                if j == 0:
                    t[lines, :] = value
                else:
                    t[lines, :] += value

    def ready():
        others(0, 4)

        @pl.when(lower)
        def _():
            f[...] = fz[mine, :]

    between = {
        4: [pre_one],
        5: [pre_cross],
        6: [pre_b1],
        7: [ready, lambda: add_block(0, 1, 1)],
        8: [lambda: add_block(1, 1, 0)],
        9: [lambda: add_block(2, 0, 0), lambda: start(c0)],
        10: [pre_j0],
        11: [pre_j1],
        12: [pre_b2],
        13: [lambda: others(4, 8)],
        14: [lambda: transposed(0)],
    }
    for i in range(4, HOPS):
        relays(i, i + 1)
        for piece in between.get(i, []):
            piece()
    for j in range(4):
        c0[j].wait_recv()
        here = quarter(half, first + 1 + j)
        w[here, :] += full[here, :]
        if j < 3:
            c1[j].start()
    transposed(1)
    others(8, 12)
    transposed(2)
    others(12, 16)
    transposed(3)

    before, after = lax.rem(z + 7, 8), lax.rem(z + 1, 8)
    position = jnp.where(k == 0, 7 - z, (z - c + 7) & 7)
    taking = (k == 1) | lower
    onward_z = jnp.where(k == 0, before, after)

    def chunk(i):
        here = pl.ds(pl.multiple_of(i * LINES, LINES), LINES)
        return push(t.at[here, :], arrived.at[here, :], ts.at[i], tr.at[i], (onward_z, x, y, k))

    def mapped(part_rows, store):
        h, l = split(part_rows)
        low = dot3((h, l), (ph[:, :BLOCK], plo[:, :BLOCK]))
        high = dot3((h[:, BLOCK:], l[:, BLOCK:]), (ph[BLOCK:, BLOCK:], plo[BLOCK:, BLOCK:]))
        for g in range(4):
            store(g, low[:, g * 128 : (g + 1) * 128])
            store(g + 4, high[:, g * 128 : (g + 1) * 128])

    def direct(i):
        @pl.when(chip_lower)
        def _():
            here = slice(i * 128, (i + 1) * 128)

            def store(g, value):
                yp[g % 2, g // 2, here, :] = value

            mapped(mf[here, :], store)

    swap = push(yp.at[1 - k], q0, a0, b0, sibling)

    def spread(d):
        return push(yp.at[k, py[d]], q1.at[d], a1.at[d], b1s.at[d], (z, x, py[d], k))

    def swap_start():
        @pl.when(chip_lower)
        def _():
            swap.start()

    def swap_end():
        @pl.when(chip_lower)
        def _():
            swap.wait()
            yp[pl.ds(k, 1)] += q0[...][None]
            for d in range(3):
                spread(d).start()

    def scatter(d, i):
        here = pl.ds(pl.multiple_of(i * 128, 128), 128)
        to = pc[d]
        return push(tq.at[to, here, :], rt.at[here, :], es.at[d, i], er.at[i], (z, x, to >> 1, to & 1))

    def last_part(i):
        here = pl.ds(pl.multiple_of(i * 128, 128), 128)

        def store(g, value):
            tq[g, here, :] = value

        mapped(t[here, :], store)
        for d in range(7):
            scatter(d, i).start()

    def chain(s):
        i = s - SKEW * position

        @pl.when(taking & (i >= 0) & (i < CHUNKS))
        def _():
            here = pl.ds(pl.multiple_of(i * LINES, LINES), LINES)

            @pl.when(position > 0)
            def _():
                chunk(i).wait_recv()
                t[here, :] += arrived[here, :]

            @pl.when(jnp.logical_not(last))
            def _():
                @pl.when(i >= 4)
                def _():
                    chunk(i - 4).wait_send()

                chunk(i).start()

            @pl.when(last & (lax.rem(i, 8) == 7))
            def _():
                last_part(i >> 3)

    def sum_one():
        finish(c1)
        w[part(at1, 768), :] += r1[0] + r1[1] + r1[2]
        start(c2)

    def sum_two():
        finish(c2)
        w[part(at2, 192), :] += r2[0] + r2[1] + r2[2]
        start(c3)

    def sum_three():
        finish(c3)
        full[part(at3, 24), :] = w[part(at3, 24), :] + (
            ((r3[0] + r3[1]) + (r3[2] + r3[3])) + ((r3[4] + r3[5]) + r3[6])
        )
        start(c4)

    def then(done, go):
        def run():
            finish(done)
            start(go)

        return run

    def gather_one():
        finish(c5)
        start(c6)
        c7[0].start()

    def gather_two():
        for d in range(3):
            c6[d].wait_recv()
            c7[d + 1].start()

    beside = {
        1: lambda: direct(0),
        4: lambda: direct(1),
        7: lambda: direct(2),
        10: lambda: direct(3),
        11: swap_start,
        9: sum_one,
        14: sum_two,
        22: swap_end,
        19: sum_three,
        28: pre_three,
        24: then(c4, c5),
        30: gather_one,
        46: gather_two,
    }

    @pl.loop(0, CHUNKS + 7 * SKEW)
    def _(s):
        chain(s)
        for at, step in beside.items():
            pl.when(s == at)(step)

    for copy in c0 + c6:
        copy.wait_send()
    finish(c7)

    def load(block):
        return split(
            jnp.concatenate([full[pl.ds(j * 1536 + block * BLOCK, BLOCK), :] for j in range(4)], axis=1)
        )

    w11, w10, w00 = load(0), load(1), load(2)
    slab = pl.ds(pl.multiple_of(c * 64, 64), 64)
    pick = jnp.where(
        lax.broadcasted_iota(jnp.int32, (BLOCK, 64), 0)
        == c * 64 + lax.broadcasted_iota(jnp.int32, (BLOCK, 64), 1),
        1.0,
        0.0,
    ).astype(BF16)

    def turned(parts):
        return tuple(dot(pick, part_of, 0, 1).astype(BF16) for part_of in parts)

    lit1, lit0 = turned(li1()), turned(li0())
    sym1 = split(symmetric(consts[1] - dot3(pair(1), w11, 0, 0)))
    inner = split(dot3(w10, pair(0)) + dot3(sym1, pair(2)))
    cl = split(consts[2] - dot3(li1(), inner, 0, 0))
    g_zero = consts[0] - dot3(pair(0), w00, 0, 0) + dot3(pair(2), w10, 0, 0) - dot2(cl, xv[...], 0, 0)
    sym0 = split(symmetric(g_zero))
    ls1 = split(dot3(lit1, sym1))
    diag_out[1] = dot3(ls1, li1())
    cross_out[...] = dot2(cgv[slab, :], li0()) - (
        dot3(split(dot3(lit1, w10)), li0()) - dot3(ls1, minus_b1())
    )
    diag_out[0] = dot3(split(dot3(lit0, sym0)), li0())

    cols = pl.ds(pl.multiple_of(c * 128, 128), 128)
    panel_out[...] = dot2(gv[...], (ph[:, cols], plo[:, cols]))

    @pl.when(chip_lower)
    def _():
        panel_out[...] -= yp[k, y]

    for d in range(3):
        @pl.when(2 * lax.rem(y + 3 - d, 4) <= z)
        def _():
            spread(d).wait_recv()
            panel_out[...] -= q1[d]

    @pl.when(last)
    def _():
        panel_out[...] -= tq[c]

    @pl.when(jnp.logical_not(last))
    def _():
        for i in range(4):
            scatter(0, i).wait_recv()
        panel_out[...] -= rt[...]

    @pl.when(last)
    def _():
        @pl.loop(0, HOPS)
        def _(i):
            beside_own(i).wait_send()
            beside_other(i).wait_send()

        for i in (HOPS - 2, HOPS - 1):
            first_hop(0, i).wait_send()
            first_hop(1, i).wait_send()

        for i in range(4):
            for d in range(7):
                scatter(d, i).wait_send()

    @pl.when(jnp.logical_not(source_chip))
    def _():
        @pl.loop(0, HOPS)
        def _(i):
            share(i).wait_send()

            @pl.when(hops < 3)
            def _():
                forward(i).wait_send()

    @pl.when(lower)
    def _():
        for d in range(3):
            across(d).wait_send()

    @pl.when(taking & jnp.logical_not(last))
    def _():
        for i in range(CHUNKS - 4, CHUNKS):
            chunk(i).wait_send()

    @pl.when(chip_lower)
    def _():
        for d in range(3):
            spread(d).wait_send()


def copy_kernel(a, b, c, out_a, out_b, out_c):
    out_a[...], out_b[...], out_c[...] = a[...], b[...], c[...]


def shards(trail, fac, xf, lf, li, grad, cg, dg):
    dma = pltpu.SemaphoreType.DMA
    anywhere = pl.BlockSpec(memory_space=pl.ANY)
    vmem = pl.BlockSpec(memory_space=pltpu.VMEM)
    shape = jax.ShapeDtypeStruct
    square = (BLOCK, BLOCK)
    results = (
        shape((BLOCK, 128), F32), shape((64, BLOCK), F32), shape((2, 64, BLOCK), F32),
    )
    made = pl.pallas_call(
        kernel,
        name="adjoint",
        out_shape=results,
        in_specs=[anywhere] * 8,
        out_specs=[vmem] * 3,
        scratch_shapes=[
            pltpu.VMEM((BLOCK, 2048), BF16),
            pltpu.VMEM((2048, 1024), BF16),
            pltpu.VMEM((BLOCK, 1024), BF16),
            pltpu.VMEM(square, BF16),
            pltpu.VMEM((2, *square), BF16),
            pltpu.VMEM((2, *square), F32),
            pltpu.VMEM(square, BF16),
            pltpu.VMEM((2, *square), BF16),
            pltpu.VMEM((2048, BLOCK), BF16),
            pltpu.VMEM((2048, 1024), BF16),
            pltpu.VMEM((BLOCK, 1024), BF16),
            pltpu.VMEM((BLOCK, 1024), F32),
            pltpu.VMEM((BLOCK, 1024), F32),
            pltpu.VMEM((BLOCK, 1024), F32),
            pltpu.VMEM((6144, 128), F32),
            pltpu.VMEM((6144, 128), F32),
            pltpu.VMEM((3, 768, 128), F32),
            pltpu.VMEM((3, 192, 128), F32),
            pltpu.VMEM((7, 24, 128), F32),
            pltpu.VMEM((1024, 1024), BF16),
            pltpu.VMEM((1024, 1024), BF16),
            pltpu.VMEM((6, *square), BF16),
            pltpu.VMEM((3, *square), F32),
            pltpu.VMEM((2, 4, BLOCK, 128), F32),
            pltpu.VMEM((4, BLOCK, 128), F32),
            pltpu.VMEM((3, BLOCK, 128), F32),
            pltpu.VMEM((8, BLOCK, 128), F32),
            pltpu.VMEM((BLOCK, 128), F32),
            dma((10,)), dma((2, HOPS)), dma((HOPS,)), dma((2, HOPS)), dma((HOPS,)), dma((3,)), dma((3,)),
            dma((4,)), dma((4,)), dma((3,)), dma((3,)), dma((3,)), dma((3,)), dma((7,)), dma((7,)),
            dma((7,)), dma((7,)), dma((3,)), dma((3,)), dma((3,)), dma((3,)), dma((4,)), dma((4,)),
            dma((CHUNKS,)), dma((CHUNKS,)), dma, dma, dma((3,)), dma((3,)), dma((7, 4)), dma((4,)),
        ],
        compiler_params=pltpu.CompilerParams(
            collective_id=0, has_side_effects=True, vmem_limit_bytes=VMEM_BYTES
        ),
    )(trail, fac, xf, lf, li, grad, cg, dg)
    return pl.pallas_call(
        copy_kernel, name="results", out_shape=results, in_specs=[vmem] * 3, out_specs=[vmem] * 3
    )(*made)


def solution(mesh):
    fine = Mesh(mesh.devices.reshape(8, 4, 4, 2), ("z", "x", "y", "k"))
    row, col = ("z", "x"), ("y", "k")
    return jax.shard_map(
        shards,
        mesh=fine,
        in_specs=(P(row, col), P(col, None), P(), P(), P(), P(row, None), P(), P()),
        out_specs=(P(row, col), P(col, None), P(None, col, None)),
        check_vma=False,
    )
```
